512 devices in a mesh: cells: 64 (over z, x), sub: 8 (over y, core).
Axes of the slice: x: 4, y: 4, z: 16, core: 2. Of those that a mesh axis runs over, the one named last changes fastest.
Arguments:
- snapshots: float32 [262144, 256], P(('cells', 'sub')), may hold values from -10 to 10, as said below
- volumes: float32 [262144], P(('cells', 'sub')), may hold values from 0.1 to 10
- live_rows: int32 [512], P(('cells', 'sub')), may hold values from 256 to 512, as said below
- probes: float32 [64, 262144], P(None, ('cells', 'sub')), may hold values from -6 to 6
Outputs:
- basis: float32 [262144, 256], P(('cells', 'sub'))
- factor: float32 [256, 256], replicated
- coefficients: float32 [64, 256], replicated
The draws below stay inside these ranges and needn't reach their ends.
Inputs may be any that keep to these rules, and one draw needn't show every extreme that they name: `live_rows`: each entry is the live row count of one device's block of 512 row slots; live rows come first in the block. Some device has all 512 live, some has 256. `snapshots`: the columns are linearly independent.
All inputs are finite; a program needn't handle non-finite values.
Results may differ from the reference program's by a relative error of at most 0.00013.
Values sent between devices are 32-bit elements; how exact they have to be, the bound alone decides.
A program may use at most 64 MiB of HBM per device.

```python
import math
import jax
import jax.numpy as jnp
from jax import lax

ROW_DEV = 512
SNAPS = 256
PROBES = 64
ROWS = 262144


def draw_snapshots(key, part):
    key_base, key_mix = jax.random.split(jax.random.fold_in(key, 11), 2)
    identity = jnp.eye(SNAPS, dtype=jnp.float32)
    base = jax.random.normal(key_base, (ROWS, SNAPS), jnp.float32)
    mixing = identity + 0.6 * jax.random.normal(key_mix, (SNAPS, SNAPS), jnp.float32) / jnp.sqrt(jnp.float32(SNAPS))
    mixed = jnp.dot(base, mixing, precision=lax.Precision.HIGHEST, preferred_element_type=jnp.float32)
    return jnp.clip(mixed, -10.0, 10.0)


def draw_live_rows(key, part):
    key_counts, key_pick = jax.random.split(jax.random.fold_in(key, 23), 2)
    blocks = ROWS // ROW_DEV
    counts = jax.random.randint(key_counts, (blocks,), ROW_DEV // 2, ROW_DEV + 1, jnp.int32)
    chosen = jax.random.randint(key_pick, (), 0, blocks, jnp.int32)
    other = (chosen + 1) % blocks
    positions = lax.iota(jnp.int32, blocks)
    counts = jnp.where(positions == chosen, ROW_DEV, counts)
    counts = jnp.where(positions == other, ROW_DEV // 2, counts)
    return counts.astype(jnp.int32)


def block_levels(own_key, dims, cuts, least, high):
    loudness = 1.0
    for position, parts in cuts:
        steps = jax.random.uniform(jax.random.fold_in(jax.random.fold_in(own_key, 6), position), (parts,), jnp.float32, least / len(cuts), high / len(cuts))
        loudness = loudness * jnp.repeat(jnp.exp(steps), dims[position] // parts).reshape((-1,) + (1,) * (len(dims) - 1 - position))
    return loudness


def gaussian(rng, extent, spread, most, cuts=(), kind=jnp.bfloat16):
    entries = jax.random.normal(rng, extent, jnp.float32) * spread
    if len(cuts) > 0:
        entries = block_levels(rng, extent, cuts, -0.22, 0.18) * entries
    return jnp.clip(entries, min=-most, max=most).astype(kind)


def setup_inputs(seed: int = 0) -> dict:
    arg_keys = jax.random.split(jax.random.key(seed), 5)
    snapshots = draw_snapshots(jax.random.fold_in(arg_keys[4], 71), 0)
    volumes = jnp.clip(jnp.exp(math.log(10.0) - 4.6051702 * jax.random.uniform(arg_keys[1], (ROWS,), jnp.float32) ** block_levels(arg_keys[1], (ROWS,), ((0, 512),), -0.2, 0.2)), 0.1, 10.0)
    live_rows = draw_live_rows(jax.random.fold_in(arg_keys[4], 71), 0)
    probes = gaussian(arg_keys[3], (PROBES, ROWS), 1.0, 6.0, ((1, 512),), jnp.float32)
    return dict(snapshots=snapshots, volumes=volumes, live_rows=live_rows, probes=probes)


HIGHEST = lax.Precision.HIGHEST

def reference(snapshots, volumes, live_rows, probes):
    total_rows = snapshots.shape[0]
    row_ids = lax.iota(jnp.int32, total_rows)
    block_ids = (row_ids // ROW_DEV).astype(jnp.int32)
    slot_ids = (row_ids % ROW_DEV).astype(jnp.int32)
    live_mask = slot_ids < live_rows[block_ids]
    row_scale = jnp.where(live_mask, jnp.sqrt(volumes), jnp.float32(0.0))
    weighted = snapshots * row_scale[:, None]
    gram_matrix = lax.dot_general(weighted.astype(jnp.float32), weighted.astype(jnp.float32), (((0,), (0,)), ((), ())), precision=HIGHEST, preferred_element_type=jnp.float32) / jnp.float32(total_rows)
    lower_factor = jnp.linalg.cholesky(gram_matrix)
    factor = lower_factor.T
    identity = jnp.eye(SNAPS, dtype=jnp.float32)
    inverse = lax.linalg.triangular_solve(factor, identity, left_side=True, lower=False)
    basis = jnp.dot(weighted.astype(jnp.float32), inverse.astype(jnp.float32), precision=HIGHEST, preferred_element_type=jnp.float32)
    probe_weighted = probes * row_scale[None, :]
    coefficients = jnp.dot(probe_weighted.astype(jnp.float32), basis.astype(jnp.float32), precision=HIGHEST, preferred_element_type=jnp.float32) / jnp.sqrt(jnp.float32(total_rows))
    return (basis, factor, coefficients)
```

```python
import jax
import jax.numpy as jnp
from jax import lax
from jax.experimental import pallas as pl
from jax.experimental.pallas import tpu as pltpu
from jax.sharding import PartitionSpec as P

HIGHEST = lax.Precision.HIGHEST
MESH = pl.DeviceIdType.MESH
F32 = jnp.float32

ORDER = 256
HALF = 128
TILE = 8
TILES = ORDER // TILE
XS = 4
SUBS = 8
PLANE = XS * SUBS
DEPTH = 16


def row_scale(volumes_ref, live_ref):
    rows = volumes_ref.shape[1]
    slots = lax.broadcasted_iota(jnp.int32, (1, rows), 1)
    return jnp.where(slots < live_ref[0], jnp.sqrt(volumes_ref[...]), 0.0)


def column_scale(scale):
    rows = scale.shape[1]
    return jnp.transpose(jnp.broadcast_to(scale, (HALF, rows)))


def scaled_rows(snap_ref, columns, weighted_ref):
    for half in range(2):
        part = slice(HALF * half, HALF * half + HALF)
        weighted_ref[:, part] = snap_ref[:, part] * columns


def reduce_kernel(
    total_rows,
    snap_ref,
    vol_ref,
    live_ref,
    probe_ref,
    out_ref,
    weighted,
    local,
    plane_buf,
    depth_buf,
    full,
    plane_send,
    plane_recv,
    depth_send,
    depth_recv,
    full_send,
    full_recv,
):
    cells = lax.axis_index("cells")
    sub = lax.axis_index("sub")
    z = cells // XS
    x = cells % XS
    me = x * SUBS + sub

    def plane_id(place):
        return (z * XS + place // SUBS, place % SUBS)

    def depth_id(place):
        return (place * XS + x, sub)

    barrier = pltpu.get_barrier_semaphore()

    def greet_depth(step, carry):
        other = (z + DEPTH // 2 + step) % DEPTH

        @pl.when(other != z)
        def _():
            pl.semaphore_signal(
                barrier, inc=1, device_id=depth_id(other), device_id_type=MESH
            )

        return carry

    def greet_plane(step, carry):
        other = (me + step) % PLANE
        pl.semaphore_signal(
            barrier, inc=1, device_id=plane_id(other), device_id_type=MESH
        )
        return carry

    lax.fori_loop(0, DEPTH, greet_depth, 0)
    lax.fori_loop(1, PLANE, greet_plane, 0)

    scale = row_scale(vol_ref, live_ref)
    scaled_rows(snap_ref, column_scale(scale), weighted)
    probe_weighted = probe_ref[...] * scale

    def gram(left, right):
        return lax.dot_general(
            left,
            right,
            (((0,), (0,)), ((), ())),
            precision=HIGHEST,
            preferred_element_type=F32,
        ) * F32(1.0 / total_rows)

    local[0:HALF, :] = gram(weighted[:, 0:HALF], weighted[...])
    local[HALF:ORDER, HALF:ORDER] = gram(
        weighted[:, HALF:ORDER], weighted[:, HALF:ORDER]
    )
    cross = jnp.dot(
        probe_weighted, weighted[...], precision=HIGHEST, preferred_element_type=F32
    )
    count = cross.shape[0]
    local[HALF : HALF + count, 0:HALF] = cross[:, 0:HALF]
    local[HALF + count : HALF + 2 * count, 0:HALF] = cross[:, HALF:ORDER]

    pl.semaphore_wait(barrier, PLANE - 1 + DEPTH - 1)

    def plane_copy(other, mine):
        return pltpu.make_async_remote_copy(
            src_ref=local.at[pl.ds(pl.multiple_of(other * TILE, TILE), TILE), :],
            dst_ref=plane_buf.at[mine],
            send_sem=plane_send.at[other],
            recv_sem=plane_recv.at[mine],
            device_id=plane_id(other),
            device_id_type=MESH,
        )

    def start_plane(step, carry):
        plane_copy((me + step) % PLANE, me).start()
        return carry

    lax.fori_loop(1, PLANE, start_plane, 0)
    total = local[pl.ds(pl.multiple_of(me * TILE, TILE), TILE), :]

    def take_plane(step, total):
        other = (me + PLANE - step) % PLANE
        pltpu.make_async_copy(
            plane_buf.at[other], plane_buf.at[other], plane_recv.at[other]
        ).wait()
        return total + plane_buf[other]

    total = lax.fori_loop(1, PLANE, take_plane, total)

    depth_buf[z] = total

    def depth_copy(other):
        return pltpu.make_async_remote_copy(
            src_ref=depth_buf.at[z],
            dst_ref=depth_buf.at[z],
            send_sem=depth_send.at[other],
            recv_sem=depth_recv.at[z],
            device_id=depth_id(other),
            device_id_type=MESH,
        )

    def start_depth(step, carry):
        far = DEPTH // 2
        depth_copy((z + DEPTH + far - (step + 1) // 2 * (1 - step % 2 * 2)) % DEPTH).start()
        return carry

    lax.fori_loop(0, DEPTH - 1, start_depth, 0)

    def wait_depth(step, carry):
        other = (z + step) % DEPTH
        pltpu.make_async_copy(
            depth_buf.at[other], depth_buf.at[other], depth_recv.at[other]
        ).wait()
        return carry

    lax.fori_loop(1, DEPTH, wait_depth, 0)
    summed = depth_buf[0]
    for place in range(1, DEPTH):
        summed = summed + depth_buf[place]

    mine = pl.ds(pl.multiple_of(me * TILE, TILE), TILE)
    full[mine, :] = summed

    def full_copy(other):
        return pltpu.make_async_remote_copy(
            src_ref=full.at[mine, :],
            dst_ref=full.at[mine, :],
            send_sem=full_send.at[other],
            recv_sem=full_recv.at[me],
            device_id=plane_id(other),
            device_id_type=MESH,
        )

    def start_full(step, carry):
        full_copy((me + step) % PLANE).start()
        return carry

    lax.fori_loop(1, PLANE, start_full, 0)

    def wait_full(step, carry):
        other = (me + PLANE - step) % PLANE
        tile = full.at[pl.ds(pl.multiple_of(other * TILE, TILE), TILE), :]
        pltpu.make_async_copy(tile, tile, full_recv.at[other]).wait()
        return carry

    lax.fori_loop(1, PLANE, wait_full, 0)

    def drain_plane(step, carry):
        other = (me + step) % PLANE
        plane_copy(other, me).wait_send()
        full_copy(other).wait_send()
        return carry

    lax.fori_loop(1, PLANE, drain_plane, 0)

    def drain_depth(step, carry):
        depth_copy((z + step) % DEPTH).wait_send()
        return carry

    lax.fori_loop(1, DEPTH, drain_depth, 0)
    out_ref[...] = full[...]


def lane_spread(block, lane):
    return jnp.broadcast_to(block[:, lane : lane + 1], (TILE, HALF))


def row_spread(block, row):
    return jnp.broadcast_to(block[row : row + 1, :], (TILE, HALF))


def eliminate(work, upper, lower_inverse):
    lane = lax.broadcasted_iota(jnp.int32, (TILE, HALF), 1)
    row_in = lax.broadcasted_iota(jnp.int32, (TILE, HALF), 0)
    diag = [lane_spread(work[0:TILE, 0:HALF], j) for j in range(TILE)]
    for t in range(TILES):
        half, low = divmod(TILE * t, HALF)
        rows_t = slice(TILE * t, TILE * t + TILE)
        current = [work[rows_t, 0:HALF], work[rows_t, HALF:ORDER]]
        unit = jnp.where(lane == low + row_in, 1.0, 0.0)
        inside = (lane >= low) & (lane < low + TILE)
        last = t == TILES - 1
        if not last:
            rows_n = slice(TILE * t + TILE, TILE * t + 2 * TILE)
            after = [work[rows_n, 0:HALF], work[rows_n, HALF:ORDER]]
            half_n, low_n = divmod(TILE * t + TILE, HALF)
            diag_n = [lane_spread(after[half_n], low_n + j) for j in range(TILE)]
            below = [lane_spread(after[half], low + j) for j in range(TILE)]
        pivots, unit_pivots, factors = [], [], []
        for k in range(TILE):
            root = lax.rsqrt(row_spread(diag[k], k))
            column = diag[k] * root
            masked = jnp.where(row_in > k, column, 0.0)
            entries = {j: row_spread(column, j) for j in range(k + 1, TILE)}
            for j in range(k + 1, TILE):
                diag[j] = diag[j] - column * entries[j]
            pivot = [row_spread(current[i], k) * root for i in range(2)]
            unit_pivot = row_spread(unit, k) * root
            if k < TILE - 1:
                current = [current[i] - masked * pivot[i] for i in range(2)]
                unit = unit - masked * unit_pivot
            pivots.append(pivot)
            unit_pivots.append(unit_pivot)
            if not last:
                factor = below[k] * root
                for j in range(k + 1, TILE):
                    below[j] = below[j] - factor * entries[j]
                for j in range(TILE):
                    diag_n[j] = diag_n[j] - factor * row_spread(factor, j)
                factors.append(factor)
        done = list(pivots[0])
        unit_done = unit_pivots[0]
        for k in range(1, TILE):
            done = [jnp.where(row_in == k, pivots[k][i], done[i]) for i in range(2)]
            unit_done = jnp.where(row_in == k, unit_pivots[k], unit_done)
        for i in range(2):
            columns = slice(HALF * i, HALF * i + HALF)
            place = lane + HALF * i
            upper[rows_t, columns] = jnp.where(place >= TILE * t + row_in, done[i], 0.0)
            left = jnp.where(place < TILE * t, done[i], 0.0)
            if i == half:
                left = jnp.where(inside, unit_done, left)
            lower_inverse[rows_t, columns] = left
        if last:
            break
        for k in range(TILE):
            pivots[k][half] = jnp.where(inside, unit_pivots[k], pivots[k][half])
        after[half] = jnp.where(inside, 0.0, after[half])
        for k in range(TILE):
            after = [after[i] - factors[k] * pivots[k][i] for i in range(2)]
        work[rows_n, 0:HALF] = after[0]
        work[rows_n, HALF:ORDER] = after[1]
        diag = diag_n
        if t < TILES - 2:
            turned = {
                i: jnp.transpose(done[i]) for i in range((TILE * t + 2 * TILE) // HALF, 2)
            }
            for s in range(t + 2, TILES):
                rows_s = slice(TILE * s, TILE * s + TILE)
                i_s, low_s = divmod(TILE * s, HALF)
                multipliers = turned[i_s][low_s : low_s + TILE, :]
                tile = [work[rows_s, 0:HALF], work[rows_s, HALF:ORDER]]
                tile[half] = jnp.where(inside, 0.0, tile[half])
                for k in range(TILE):
                    spread = lane_spread(multipliers, k)
                    tile = [tile[i] - spread * pivots[k][i] for i in range(2)]
                work[rows_s, 0:HALF] = tile[0]
                work[rows_s, HALF:ORDER] = tile[1]


def finish_kernel(
    root_total,
    sums_ref,
    snap_ref,
    vol_ref,
    live_ref,
    basis_ref,
    factor_ref,
    coef_ref,
    work,
    inverse,
    weighted,
):
    count = coef_ref.shape[0]
    work[0:HALF, :] = sums_ref[0:HALF, :]
    work[HALF:ORDER, HALF:ORDER] = sums_ref[HALF:ORDER, HALF:ORDER]
    work[HALF:ORDER, 0:HALF] = jnp.transpose(sums_ref[0:HALF, HALF:ORDER])
    scale = row_scale(vol_ref, live_ref)
    scaled_rows(snap_ref, column_scale(scale), weighted)
    eliminate(work, factor_ref, inverse)

    def apply(left):
        return lax.dot_general(
            left,
            inverse[...],
            (((1,), (1,)), ((), ())),
            precision=HIGHEST,
            preferred_element_type=F32,
        )

    basis_ref[...] = apply(weighted[...])
    cross = jnp.concatenate(
        [
            sums_ref[HALF : HALF + count, 0:HALF],
            sums_ref[HALF + count : HALF + 2 * count, 0:HALF],
        ],
        axis=1,
    )
    coef_ref[...] = apply(cross) / F32(root_total)


def per_device(snapshots, volumes, live_rows, probes):
    row_count = snapshots.shape[0]
    total_rows = row_count * PLANE * DEPTH
    in_vmem = pl.BlockSpec(memory_space=pltpu.VMEM)
    in_smem = pl.BlockSpec(memory_space=pltpu.SMEM)
    volumes = volumes.reshape(1, row_count)
    dma = pltpu.SemaphoreType.DMA

    def reduce_body(*refs):
        reduce_kernel(total_rows, *refs)

    sums = pl.pallas_call(
        reduce_body,
        out_shape=jax.ShapeDtypeStruct((ORDER, ORDER), F32),
        in_specs=[in_vmem, in_vmem, in_smem, in_vmem],
        out_specs=in_vmem,
        scratch_shapes=[
            pltpu.VMEM((row_count, ORDER), F32),
            pltpu.VMEM((ORDER, ORDER), F32),
            pltpu.VMEM((PLANE, TILE, ORDER), F32),
            pltpu.VMEM((DEPTH, TILE, ORDER), F32),
            pltpu.VMEM((ORDER, ORDER), F32),
            dma((PLANE,)),
            dma((PLANE,)),
            dma((DEPTH,)),
            dma((DEPTH,)),
            dma((PLANE,)),
            dma((PLANE,)),
        ],
        compiler_params=pltpu.CompilerParams(collective_id=0, has_side_effects=True),
        name="reduce_sums",
    )(snapshots, volumes, live_rows, probes)

    def finish_body(*refs):
        finish_kernel(float(total_rows) ** 0.5, *refs)

    return pl.pallas_call(
        finish_body,
        out_shape=(
            jax.ShapeDtypeStruct((row_count, ORDER), F32),
            jax.ShapeDtypeStruct((ORDER, ORDER), F32),
            jax.ShapeDtypeStruct((probes.shape[0], ORDER), F32),
        ),
        in_specs=[in_vmem, in_vmem, in_vmem, in_smem],
        out_specs=(in_vmem, in_vmem, in_vmem),
        scratch_shapes=[
            pltpu.VMEM((ORDER, ORDER), F32),
            pltpu.VMEM((ORDER, ORDER), F32),
            pltpu.VMEM((row_count, ORDER), F32),
        ],
        name="factor_apply",
    )(sums, snapshots, volumes, live_rows)


def solution(mesh):
    both = ("cells", "sub")
    placed = (P(both, None), P(both), P(both), P(None, both))
    return jax.shard_map(
        per_device,
        mesh=mesh,
        in_specs=placed,
        out_specs=(P(both, None), P(), P()),
        check_vma=False,
    )
```

```python
import jax
import jax.numpy as jnp
from jax import lax
from jax.experimental import pallas as pl
from jax.experimental.pallas import tpu as pltpu
from jax.sharding import PartitionSpec as P

HIGHEST = lax.Precision.HIGHEST
MESH = pl.DeviceIdType.MESH
F32 = jnp.float32

ORDER = 256
HALF = 128
TILE = 8
TILES = ORDER // TILE
PANEL = 8
XS = 4
YS = 4
CORES = 2
PLANE = XS * YS
DEPTH = 16


def reduce_kernel(
    total_rows,
    snap_hbm,
    vol_hbm,
    live_hbm,
    probe_hbm,
    out_ref,
    weighted,
    snap,
    vol,
    live,
    probe,
    local,
    pair_buf,
    plane_buf,
    depth_buf,
    full,
    load_sems,
    pair_sems,
    plane_send,
    plane_recv,
    depth_send,
    depth_recv,
    full_send,
    full_recv,
    cross_send,
    cross_recv,
):
    cells = lax.axis_index("cells")
    sub = lax.axis_index("sub")
    z = cells // XS
    x = cells % XS
    y = sub // CORES
    core = sub % CORES
    me = x * YS + y

    def pair_id():
        return (cells, y * CORES + 1 - core)

    def plane_id(place):
        return (z * XS + place // YS, place % YS * CORES + core)

    def depth_id(place):
        return (place * XS + x, sub)

    loads = [
        pltpu.make_async_copy(source, target, load_sems.at[i])
        for i, (source, target) in enumerate(
            [(live_hbm, live), (vol_hbm, vol), (snap_hbm, snap), (probe_hbm, probe)]
        )
    ]
    for load in loads:
        load.start()

    barrier = pltpu.get_barrier_semaphore()

    def greet_depth(step, carry):
        pl.semaphore_signal(
            barrier,
            inc=1,
            device_id=depth_id((z + DEPTH // 2 + step) % DEPTH),
            device_id_type=MESH,
        )
        return carry

    def greet_plane(step, carry):
        pl.semaphore_signal(
            barrier,
            inc=1,
            device_id=plane_id((me + step) % PLANE),
            device_id_type=MESH,
        )
        return carry

    lax.fori_loop(0, DEPTH // 2, greet_depth, 0)
    lax.fori_loop(DEPTH // 2 + 1, DEPTH, greet_depth, 0)
    lax.fori_loop(1, PLANE, greet_plane, 0)
    pl.semaphore_signal(barrier, inc=1, device_id=pair_id(), device_id_type=MESH)

    loads[0].wait()
    loads[1].wait()
    rows = vol.shape[1]
    slots = lax.broadcasted_iota(jnp.int32, (1, rows), 1)
    scale = jnp.where(slots < live[0], jnp.sqrt(vol[...]), 0.0)
    columns = jnp.transpose(jnp.broadcast_to(scale, (HALF, rows)))
    loads[2].wait()
    for half in range(2):
        part = slice(HALF * half, HALF * half + HALF)
        weighted[:, part] = snap[:, part] * columns

    def gram(left, right):
        return lax.dot_general(
            left,
            right,
            (((0,), (0,)), ((), ())),
            precision=HIGHEST,
            preferred_element_type=F32,
        ) * F32(1.0 / total_rows)

    local[0:HALF, :] = gram(weighted[:, 0:HALF], weighted[...])
    local[HALF:ORDER, HALF:ORDER] = gram(
        weighted[:, HALF:ORDER], weighted[:, HALF:ORDER]
    )
    loads[3].wait()
    cross = jnp.dot(
        probe[...] * scale, weighted[...], precision=HIGHEST, preferred_element_type=F32
    )
    count = cross.shape[0]
    local[HALF : HALF + count, 0:HALF] = cross[:, 0:HALF]
    local[HALF + count : HALF + 2 * count, 0:HALF] = cross[:, HALF:ORDER]

    pl.semaphore_wait(barrier, 1 + PLANE - 1 + DEPTH - 1)

    def half_rows(which):
        return pl.ds(pl.multiple_of(which * HALF, HALF), HALF)

    pair = pltpu.make_async_remote_copy(
        src_ref=local.at[half_rows(1 - core), :],
        dst_ref=pair_buf,
        send_sem=pair_sems.at[0],
        recv_sem=pair_sems.at[1],
        device_id=pair_id(),
        device_id_type=MESH,
    )
    pair.start()
    pair.wait()
    pair_buf[...] = pair_buf[...] + local[half_rows(core), :]

    def tile_of(place):
        return pl.ds(pl.multiple_of(place * TILE, TILE), TILE)

    def plane_copy(other):
        return pltpu.make_async_remote_copy(
            src_ref=pair_buf.at[tile_of(other), :],
            dst_ref=plane_buf.at[me],
            send_sem=plane_send.at[other],
            recv_sem=plane_recv.at[me],
            device_id=plane_id(other),
            device_id_type=MESH,
        )

    def start_plane(step, carry):
        plane_copy((me + step) % PLANE).start()
        return carry

    lax.fori_loop(1, PLANE, start_plane, 0)

    def take_plane(step, total):
        other = (me + PLANE - step) % PLANE
        pltpu.make_async_copy(
            plane_buf.at[other], plane_buf.at[other], plane_recv.at[other]
        ).wait()
        return total + plane_buf[other]

    total = lax.fori_loop(1, PLANE, take_plane, pair_buf[tile_of(me), :])

    depth_buf[z] = total

    def depth_copy(other):
        return pltpu.make_async_remote_copy(
            src_ref=depth_buf.at[z],
            dst_ref=depth_buf.at[z],
            send_sem=depth_send.at[other],
            recv_sem=depth_recv.at[z],
            device_id=depth_id(other),
            device_id_type=MESH,
        )

    def start_depth(step, carry):
        far = DEPTH // 2
        near = (step + 1) // 2 * (1 - step % 2 * 2)
        depth_copy((z + DEPTH + far - near) % DEPTH).start()
        return carry

    lax.fori_loop(0, DEPTH - 1, start_depth, 0)

    def wait_depth(step, carry):
        other = (z + step) % DEPTH
        pltpu.make_async_copy(
            depth_buf.at[other], depth_buf.at[other], depth_recv.at[other]
        ).wait()
        return carry

    lax.fori_loop(1, DEPTH, wait_depth, 0)
    summed = depth_buf[0]
    for place in range(1, DEPTH):
        summed = summed + depth_buf[place]

    def own_tile(place):
        return pl.ds(pl.multiple_of(core * HALF + place * TILE, TILE), TILE)

    full[own_tile(me), :] = summed

    def full_copy(other):
        return pltpu.make_async_remote_copy(
            src_ref=full.at[own_tile(me), :],
            dst_ref=full.at[own_tile(me), :],
            send_sem=full_send.at[other],
            recv_sem=full_recv.at[me],
            device_id=plane_id(other),
            device_id_type=MESH,
        )

    def cross_copy(place):
        return pltpu.make_async_remote_copy(
            src_ref=full.at[own_tile(place), :],
            dst_ref=full.at[own_tile(place), :],
            send_sem=cross_send.at[place],
            recv_sem=cross_recv.at[place],
            device_id=pair_id(),
            device_id_type=MESH,
        )

    def start_full(step, carry):
        full_copy((me + step) % PLANE).start()
        return carry

    lax.fori_loop(1, PLANE, start_full, 0)
    cross_copy(me).start()

    def hand_on(step, carry):
        other = (me + PLANE - step) % PLANE
        tile = full.at[own_tile(other), :]
        pltpu.make_async_copy(tile, tile, full_recv.at[other]).wait()
        cross_copy(other).start()
        return carry

    lax.fori_loop(1, PLANE, hand_on, 0)

    def drain(step, carry):
        other = (me + step) % PLANE
        plane_copy(other).wait_send()
        full_copy(other).wait_send()
        return carry

    lax.fori_loop(1, PLANE, drain, 0)

    def drain_depth(step, carry):
        depth_copy((z + step) % DEPTH).wait_send()
        return carry

    lax.fori_loop(1, DEPTH, drain_depth, 0)

    def wait_cross(place, carry):
        cross_copy(place).wait_send()
        tile = full.at[
            pl.ds(pl.multiple_of((1 - core) * HALF + place * TILE, TILE), TILE), :
        ]
        pltpu.make_async_copy(tile, tile, cross_recv.at[place]).wait()
        return carry

    lax.fori_loop(0, PLANE, wait_cross, 0)
    out_ref[...] = full[...]


def lane_spread(block, lane):
    return jnp.broadcast_to(block[:, lane : lane + 1], (TILE, HALF))


def row_spread(block, row):
    return jnp.broadcast_to(block[row : row + 1, :], (TILE, HALF))


def stack_rows(row_in, rows):
    stacked = rows[0]
    for k in range(1, TILE):
        stacked = jnp.where(row_in == k, rows[k], stacked)
    return stacked


def eliminate(work, upper, lower_inverse, panel_rows):
    lane = lax.broadcasted_iota(jnp.int32, (TILE, HALF), 1)
    row_in = lax.broadcasted_iota(jnp.int32, (TILE, HALF), 0)
    for t in range(TILES):
        end = (t // PANEL + 1) * PANEL
        half, low = divmod(TILE * t, HALF)
        rows_t = slice(TILE * t, TILE * t + TILE)
        current = [work[rows_t, 0:HALF], work[rows_t, HALF:ORDER]]
        if t % PANEL == 0:
            diag = [lane_spread(current[half], low + j) for j in range(TILE)]
        unit = jnp.where(lane == low + row_in, 1.0, 0.0)
        inside = (lane >= low) & (lane < low + TILE)
        last = t == end - 1
        if not last:
            rows_n = slice(TILE * t + TILE, TILE * t + 2 * TILE)
            after = [work[rows_n, 0:HALF], work[rows_n, HALF:ORDER]]
            half_n, low_n = divmod(TILE * t + TILE, HALF)
            diag_n = [lane_spread(after[half_n], low_n + j) for j in range(TILE)]
            below = [lane_spread(after[half], low + j) for j in range(TILE)]
        pivots, unit_pivots, factors = [], [], []
        for k in range(TILE):
            root = lax.rsqrt(row_spread(diag[k], k))
            column = diag[k] * root
            masked = jnp.where(row_in > k, column, 0.0)
            entries = {j: row_spread(column, j) for j in range(k + 1, TILE)}
            for j in range(k + 1, TILE):
                diag[j] = diag[j] - column * entries[j]
            pivot = [row_spread(current[i], k) * root for i in range(2)]
            unit_pivot = row_spread(unit, k) * root
            if k < TILE - 1:
                current = [current[i] - masked * pivot[i] for i in range(2)]
                unit = unit - masked * unit_pivot
            pivots.append(pivot)
            unit_pivots.append(unit_pivot)
            if not last:
                factor = below[k] * root
                for j in range(k + 1, TILE):
                    below[j] = below[j] - factor * entries[j]
                for j in range(TILE):
                    diag_n[j] = diag_n[j] - factor * row_spread(factor, j)
                factors.append(factor)
        own = stack_rows(row_in, [pivots[k][half] for k in range(TILE)])
        for k in range(TILE):
            pivots[k][half] = jnp.where(inside, unit_pivots[k], pivots[k][half])
        done = [
            stack_rows(row_in, [pivots[k][i] for k in range(TILE)]) for i in range(2)
        ]
        for i in range(2):
            columns = slice(HALF * i, HALF * i + HALF)
            place = lane + HALF * i
            lower_inverse[rows_t, columns] = jnp.where(
                place < TILE * t + TILE, done[i], 0.0
            )
            shown = jnp.where(inside, own, done[i]) if i == half else done[i]
            upper[rows_t, columns] = jnp.where(place >= TILE * t + row_in, shown, 0.0)
            panel_rows[TILE * (t % PANEL) : TILE * (t % PANEL) + TILE, columns] = (
                jnp.where(
                    (place >= TILE * t + TILE) & (place < TILE * end), 0.0, done[i]
                )
            )
        if not last:
            after[half] = jnp.where(inside, 0.0, after[half])
            for k in range(TILE):
                after = [after[i] - factors[k] * pivots[k][i] for i in range(2)]
            work[rows_n, 0:HALF] = after[0]
            work[rows_n, HALF:ORDER] = after[1]
            diag = diag_n
            rest = range(t + 2, end)
            if len(rest) > 0:
                halves = range((TILE * t + 2 * TILE) // HALF, (TILE * end - 1) // HALF + 1)
                turned = {i: jnp.transpose(done[i]) for i in halves}
                tiles = {}
                for s in rest:
                    rows_s = slice(TILE * s, TILE * s + TILE)
                    tiles[s] = [work[rows_s, 0:HALF], work[rows_s, HALF:ORDER]]
                    tiles[s][half] = jnp.where(inside, 0.0, tiles[s][half])
                for k in range(TILE):
                    for s in rest:
                        i_s, low_s = divmod(TILE * s, HALF)
                        spread = lane_spread(turned[i_s][low_s : low_s + TILE, :], k)
                        tiles[s] = [
                            tiles[s][i] - spread * pivots[k][i] for i in range(2)
                        ]
                for s in rest:
                    rows_s = slice(TILE * s, TILE * s + TILE)
                    work[rows_s, 0:HALF] = tiles[s][0]
                    work[rows_s, HALF:ORDER] = tiles[s][1]
        elif end < TILES:
            reached = TILE * end
            first = reached - TILE * PANEL
            turned = jnp.transpose(panel_rows[...])
            update = jnp.dot(
                turned[reached:, :],
                panel_rows[...],
                precision=HIGHEST,
                preferred_element_type=F32,
            )
            place = lax.broadcasted_iota(jnp.int32, (ORDER - reached, ORDER), 1)
            in_panel = (place >= first) & (place < reached)
            work[reached:, :] = jnp.where(in_panel, 0.0, work[reached:, :]) - update


def finish_kernel(
    root_total,
    sums_ref,
    weighted,
    basis_hbm,
    factor_hbm,
    coef_hbm,
    work,
    upper,
    inverse,
    panel_rows,
    basis,
    coef,
    sems,
):
    count = coef.shape[0]
    work[0:HALF, :] = sums_ref[0:HALF, :]
    work[HALF:ORDER, HALF:ORDER] = sums_ref[HALF:ORDER, HALF:ORDER]
    work[HALF:ORDER, 0:HALF] = jnp.transpose(sums_ref[0:HALF, HALF:ORDER])
    eliminate(work, upper, inverse, panel_rows)
    copies = [pltpu.make_async_copy(upper, factor_hbm, sems.at[0])]
    copies[0].start()

    def apply(left):
        return lax.dot_general(
            left,
            inverse[...],
            (((1,), (1,)), ((), ())),
            precision=HIGHEST,
            preferred_element_type=F32,
        )

    cross = jnp.concatenate(
        [
            sums_ref[HALF : HALF + count, 0:HALF],
            sums_ref[HALF + count : HALF + 2 * count, 0:HALF],
        ],
        axis=1,
    )
    coef[...] = apply(cross) / F32(root_total)
    copies.append(pltpu.make_async_copy(coef, coef_hbm, sems.at[1]))
    copies[1].start()
    for part in range(basis.shape[0] // HALF):
        rows = slice(HALF * part, HALF * part + HALF)
        basis[rows, :] = apply(weighted[rows, :])
        copies.append(
            pltpu.make_async_copy(
                basis.at[rows, :], basis_hbm.at[rows, :], sems.at[2 + part]
            )
        )
        copies[-1].start()
    for copy in copies:
        copy.wait()


def per_device(snapshots, volumes, live_rows, probes):
    row_count = snapshots.shape[0]
    count = probes.shape[0]
    total_rows = row_count * CORES * PLANE * DEPTH
    in_vmem = pl.BlockSpec(memory_space=pltpu.VMEM)
    anywhere = pl.BlockSpec(memory_space=pl.ANY)
    volumes = volumes.reshape(1, row_count)
    dma = pltpu.SemaphoreType.DMA

    def reduce_body(*refs):
        reduce_kernel(total_rows, *refs)

    sums, weighted = pl.pallas_call(
        reduce_body,
        out_shape=(
            pltpu.VMEM((ORDER, ORDER), F32),
            pltpu.VMEM((row_count, ORDER), F32),
        ),
        in_specs=[pl.BlockSpec(memory_space=pltpu.HBM)] * 4,
        out_specs=(in_vmem, in_vmem),
        scratch_shapes=[
            pltpu.VMEM((row_count, ORDER), F32),
            pltpu.VMEM((1, row_count), F32),
            pltpu.SMEM((1,), jnp.int32),
            pltpu.VMEM((count, row_count), F32),
            pltpu.VMEM((ORDER, ORDER), F32),
            pltpu.VMEM((HALF, ORDER), F32),
            pltpu.VMEM((PLANE, TILE, ORDER), F32),
            pltpu.VMEM((DEPTH, TILE, ORDER), F32),
            pltpu.VMEM((ORDER, ORDER), F32),
            dma((4,)),
            dma((2,)),
            dma((PLANE,)),
            dma((PLANE,)),
            dma((DEPTH,)),
            dma((DEPTH,)),
            dma((PLANE,)),
            dma((PLANE,)),
            dma((PLANE,)),
            dma((PLANE,)),
        ],
        compiler_params=pltpu.CompilerParams(collective_id=0, has_side_effects=True),
        name="reduce_sums",
    )(snapshots, volumes, live_rows, probes)

    def finish_body(*refs):
        finish_kernel(float(total_rows) ** 0.5, *refs)

    return pl.pallas_call(
        finish_body,
        out_shape=(
            jax.ShapeDtypeStruct((row_count, ORDER), F32),
            jax.ShapeDtypeStruct((ORDER, ORDER), F32),
            jax.ShapeDtypeStruct((count, ORDER), F32),
        ),
        in_specs=[in_vmem, in_vmem],
        out_specs=(anywhere, anywhere, anywhere),
        scratch_shapes=[
            pltpu.VMEM((ORDER, ORDER), F32),
            pltpu.VMEM((ORDER, ORDER), F32),
            pltpu.VMEM((ORDER, ORDER), F32),
            pltpu.VMEM((TILE * PANEL, ORDER), F32),
            pltpu.VMEM((row_count, ORDER), F32),
            pltpu.VMEM((count, ORDER), F32),
            dma((2 + row_count // HALF,)),
        ],
        name="factor_apply",
    )(
        pltpu.with_memory_space_constraint(sums, pltpu.VMEM),
        pltpu.with_memory_space_constraint(weighted, pltpu.VMEM),
    )


def solution(mesh):
    both = ("cells", "sub")
    placed = (P(both, None), P(both), P(both), P(None, both))
    return jax.shard_map(
        per_device,
        mesh=mesh,
        in_specs=placed,
        out_specs=(P(both, None), P(), P()),
        check_vma=False,
    )
```

```python
import jax
import jax.numpy as jnp
from jax import lax
from jax.experimental import pallas as pl
from jax.experimental.pallas import tpu as pltpu
from jax.sharding import PartitionSpec as P

HIGHEST = lax.Precision.HIGHEST
MESH = pl.DeviceIdType.MESH
F32 = jnp.float32

ORDER = 256
HALF = 128
TILE = 8
TILES = ORDER // TILE
PANEL = 8
XS = 4
YS = 4
CORES = 2
PLANE = XS * YS
DEPTH = 16
RELAYS = (1, 2, 4)


def plane_offsets():
    places = [(dx, dy) for dx in range(XS) for dy in range(YS)]
    hops = lambda place: sum(min(d, 4 - d) for d in place)
    return sorted(places, key=hops, reverse=True)[:-1]


def reduce_kernel(
    total_rows,
    snap_hbm,
    vol_hbm,
    live_hbm,
    probe_hbm,
    out_ref,
    weighted,
    snap,
    vol,
    live,
    probe,
    local,
    pair_buf,
    plane_buf,
    depth_buf,
    full,
    load_sems,
    relay_sems,
    pair_sems,
    plane_send,
    plane_recv,
    depth_send,
    depth_recv,
    full_send,
    full_recv,
    cross_send,
    cross_recv,
):
    cells = lax.axis_index("cells")
    sub = lax.axis_index("sub")
    z = cells // XS
    x = cells % XS
    y = sub // CORES
    core = sub % CORES
    me = x * YS + y

    def pair_id():
        return (cells, y * CORES + 1 - core)

    def plane_id(place):
        return (z * XS + place // YS, place % YS * CORES + core)

    def depth_id(place):
        return (place * XS + x, sub)

    targets = [(x + dx) % XS * YS + (y + dy) % YS for dx, dy in plane_offsets()]
    sources = [
        (x + XS - dx) % XS * YS + (y + YS - dy) % YS
        for dx, dy in reversed(plane_offsets())
    ]

    def signal(sem, device):
        pl.semaphore_signal(sem, inc=1, device_id=device, device_id_type=MESH)

    def relay(stage):
        for step in (RELAYS[stage], DEPTH - RELAYS[stage]):
            signal(relay_sems.at[stage], depth_id((z + step) % DEPTH))

    loads = [
        pltpu.make_async_copy(source, target, load_sems.at[i])
        for i, (source, target) in enumerate(
            [(live_hbm, live), (vol_hbm, vol), (snap_hbm, snap), (probe_hbm, probe)]
        )
    ]
    for load in loads:
        load.start()

    barrier = pltpu.get_barrier_semaphore()
    for other in targets:
        signal(barrier, plane_id(other))
    for step in (1, DEPTH - 1):
        signal(barrier, depth_id((z + step) % DEPTH))
    signal(barrier, pair_id())

    loads[0].wait()
    loads[1].wait()
    rows = vol.shape[1]
    slots = lax.broadcasted_iota(jnp.int32, (1, rows), 1)
    scale = jnp.where(slots < live[0], jnp.sqrt(vol[...]), 0.0)
    columns = jnp.transpose(jnp.broadcast_to(scale, (HALF, rows)))
    loads[2].wait()
    for half in range(2):
        part = slice(HALF * half, HALF * half + HALF)
        weighted[:, part] = snap[:, part] * columns

    def gram(left, right):
        return lax.dot_general(
            left,
            right,
            (((0,), (0,)), ((), ())),
            precision=HIGHEST,
            preferred_element_type=F32,
        ) * F32(1.0 / total_rows)

    local[0:HALF, :] = gram(weighted[:, 0:HALF], weighted[...])
    local[HALF:ORDER, HALF:ORDER] = gram(
        weighted[:, HALF:ORDER], weighted[:, HALF:ORDER]
    )
    loads[3].wait()
    cross = jnp.dot(
        probe[...] * scale, weighted[...], precision=HIGHEST, preferred_element_type=F32
    )
    count = cross.shape[0]
    local[HALF : HALF + count, 0:HALF] = cross[:, 0:HALF]
    local[HALF + count : HALF + 2 * count, 0:HALF] = cross[:, HALF:ORDER]

    pl.semaphore_wait(barrier, 1 + PLANE - 1 + 2)
    relay(0)

    def half_rows(which):
        return pl.ds(pl.multiple_of(which * HALF, HALF), HALF)

    pair = pltpu.make_async_remote_copy(
        src_ref=local.at[half_rows(1 - core), :],
        dst_ref=pair_buf,
        send_sem=pair_sems.at[0],
        recv_sem=pair_sems.at[1],
        device_id=pair_id(),
        device_id_type=MESH,
    )
    pair.start()
    pl.semaphore_wait(relay_sems.at[0], 2)
    relay(1)
    pair.wait()
    pair_buf[...] = pair_buf[...] + local[half_rows(core), :]

    def tile_of(place):
        return pl.ds(pl.multiple_of(place * TILE, TILE), TILE)

    def plane_copy(other):
        return pltpu.make_async_remote_copy(
            src_ref=pair_buf.at[tile_of(other), :],
            dst_ref=plane_buf.at[me],
            send_sem=plane_send.at[other],
            recv_sem=plane_recv.at[me],
            device_id=plane_id(other),
            device_id_type=MESH,
        )

    for other in targets:
        plane_copy(other).start()
    pl.semaphore_wait(relay_sems.at[1], 2)
    relay(2)
    total = pair_buf[tile_of(me), :]
    for other in sources:
        pltpu.make_async_copy(
            plane_buf.at[other], plane_buf.at[other], plane_recv.at[other]
        ).wait()
        total = total + plane_buf[other]

    depth_buf[z] = total

    def depth_copy(other):
        return pltpu.make_async_remote_copy(
            src_ref=depth_buf.at[z],
            dst_ref=depth_buf.at[z],
            send_sem=depth_send.at[other],
            recv_sem=depth_recv.at[z],
            device_id=depth_id(other),
            device_id_type=MESH,
        )

    def start_depth(step, carry):
        far = DEPTH // 2
        near = (step + 1) // 2 * (1 - step % 2 * 2)
        depth_copy((z + DEPTH + far - near) % DEPTH).start()
        return carry

    pl.semaphore_wait(relay_sems.at[2], 2)
    lax.fori_loop(0, DEPTH - 1, start_depth, 0)

    def wait_depth(step, carry):
        other = (z + step) % DEPTH
        pltpu.make_async_copy(
            depth_buf.at[other], depth_buf.at[other], depth_recv.at[other]
        ).wait()
        return carry

    lax.fori_loop(1, DEPTH, wait_depth, 0)
    summed = depth_buf[0]
    for place in range(1, DEPTH):
        summed = summed + depth_buf[place]

    def own_tile(place):
        return pl.ds(pl.multiple_of(core * HALF + place * TILE, TILE), TILE)

    full[own_tile(me), :] = summed

    def full_copy(other):
        return pltpu.make_async_remote_copy(
            src_ref=full.at[own_tile(me), :],
            dst_ref=full.at[own_tile(me), :],
            send_sem=full_send.at[other],
            recv_sem=full_recv.at[me],
            device_id=plane_id(other),
            device_id_type=MESH,
        )

    def cross_copy(place):
        return pltpu.make_async_remote_copy(
            src_ref=full.at[own_tile(place), :],
            dst_ref=full.at[own_tile(place), :],
            send_sem=cross_send.at[place],
            recv_sem=cross_recv.at[place],
            device_id=pair_id(),
            device_id_type=MESH,
        )

    for other in targets:
        full_copy(other).start()
    cross_copy(me).start()
    for other in sources:
        tile = full.at[own_tile(other), :]
        pltpu.make_async_copy(tile, tile, full_recv.at[other]).wait()
        cross_copy(other).start()

    def drain(step, carry):
        other = (me + step) % PLANE
        plane_copy(other).wait_send()
        full_copy(other).wait_send()
        return carry

    lax.fori_loop(1, PLANE, drain, 0)

    def drain_depth(step, carry):
        depth_copy((z + step) % DEPTH).wait_send()
        return carry

    lax.fori_loop(1, DEPTH, drain_depth, 0)

    def wait_cross(place, carry):
        cross_copy(place).wait_send()
        tile = full.at[
            pl.ds(pl.multiple_of((1 - core) * HALF + place * TILE, TILE), TILE), :
        ]
        pltpu.make_async_copy(tile, tile, cross_recv.at[place]).wait()
        return carry

    lax.fori_loop(0, PLANE, wait_cross, 0)
    out_ref[...] = full[...]


def lane_spread(block, lane):
    return jnp.broadcast_to(block[:, lane : lane + 1], (TILE, HALF))


def row_spread(block, row):
    return jnp.broadcast_to(block[row : row + 1, :], (TILE, HALF))


def stack_rows(row_in, rows):
    stacked = rows[0]
    for k in range(1, TILE):
        stacked = jnp.where(row_in == k, rows[k], stacked)
    return stacked


def eliminate(work, upper, lower_inverse, panel_rows):
    lane = lax.broadcasted_iota(jnp.int32, (TILE, HALF), 1)
    row_in = lax.broadcasted_iota(jnp.int32, (TILE, HALF), 0)
    for t in range(TILES):
        end = (t // PANEL + 1) * PANEL
        half, low = divmod(TILE * t, HALF)
        rows_t = slice(TILE * t, TILE * t + TILE)
        current = [work[rows_t, 0:HALF], work[rows_t, HALF:ORDER]]
        if t % PANEL == 0:
            diag = [lane_spread(current[half], low + j) for j in range(TILE)]
        unit = jnp.where(lane == low + row_in, 1.0, 0.0)
        inside = (lane >= low) & (lane < low + TILE)
        last = t == end - 1
        if not last:
            rows_n = slice(TILE * t + TILE, TILE * t + 2 * TILE)
            after = [work[rows_n, 0:HALF], work[rows_n, HALF:ORDER]]
            half_n, low_n = divmod(TILE * t + TILE, HALF)
            diag_n = [lane_spread(after[half_n], low_n + j) for j in range(TILE)]
            below = [lane_spread(after[half], low + j) for j in range(TILE)]
        pivots, unit_pivots, factors = [], [], []
        for k in range(TILE):
            root = lax.rsqrt(row_spread(diag[k], k))
            column = diag[k] * root
            masked = jnp.where(row_in > k, column, 0.0)
            entries = {j: row_spread(column, j) for j in range(k + 1, TILE)}
            for j in range(k + 1, TILE):
                diag[j] = diag[j] - column * entries[j]
            pivot = [row_spread(current[i], k) * root for i in range(2)]
            unit_pivot = row_spread(unit, k) * root
            if k < TILE - 1:
                current = [current[i] - masked * pivot[i] for i in range(2)]
                unit = unit - masked * unit_pivot
            pivots.append(pivot)
            unit_pivots.append(unit_pivot)
            if not last:
                factor = below[k] * root
                for j in range(k + 1, TILE):
                    below[j] = below[j] - factor * entries[j]
                for j in range(TILE):
                    diag_n[j] = diag_n[j] - factor * row_spread(factor, j)
                factors.append(factor)
        own = stack_rows(row_in, [pivots[k][half] for k in range(TILE)])
        for k in range(TILE):
            pivots[k][half] = jnp.where(inside, unit_pivots[k], pivots[k][half])
        done = [
            stack_rows(row_in, [pivots[k][i] for k in range(TILE)]) for i in range(2)
        ]
        for i in range(2):
            columns = slice(HALF * i, HALF * i + HALF)
            place = lane + HALF * i
            lower_inverse[rows_t, columns] = jnp.where(
                place < TILE * t + TILE, done[i], 0.0
            )
            shown = jnp.where(inside, own, done[i]) if i == half else done[i]
            upper[rows_t, columns] = jnp.where(place >= TILE * t + row_in, shown, 0.0)
            panel_rows[TILE * (t % PANEL) : TILE * (t % PANEL) + TILE, columns] = (
                jnp.where(
                    (place >= TILE * t + TILE) & (place < TILE * end), 0.0, done[i]
                )
            )
        if not last:
            after[half] = jnp.where(inside, 0.0, after[half])
            for k in range(TILE):
                after = [after[i] - factors[k] * pivots[k][i] for i in range(2)]
            work[rows_n, 0:HALF] = after[0]
            work[rows_n, HALF:ORDER] = after[1]
            diag = diag_n
            rest = range(t + 2, end)
            if len(rest) > 0:
                halves = range((TILE * t + 2 * TILE) // HALF, (TILE * end - 1) // HALF + 1)
                turned = {i: jnp.transpose(done[i]) for i in halves}
                tiles = {}
                for s in rest:
                    rows_s = slice(TILE * s, TILE * s + TILE)
                    tiles[s] = [work[rows_s, 0:HALF], work[rows_s, HALF:ORDER]]
                    tiles[s][half] = jnp.where(inside, 0.0, tiles[s][half])
                for k in range(TILE):
                    for s in rest:
                        i_s, low_s = divmod(TILE * s, HALF)
                        spread = lane_spread(turned[i_s][low_s : low_s + TILE, :], k)
                        tiles[s] = [
                            tiles[s][i] - spread * pivots[k][i] for i in range(2)
                        ]
                for s in rest:
                    rows_s = slice(TILE * s, TILE * s + TILE)
                    work[rows_s, 0:HALF] = tiles[s][0]
                    work[rows_s, HALF:ORDER] = tiles[s][1]
        elif end < TILES:
            reached = TILE * end
            first = reached - TILE * PANEL
            turned = jnp.transpose(panel_rows[...])
            update = jnp.dot(
                turned[reached:, :],
                panel_rows[...],
                precision=HIGHEST,
                preferred_element_type=F32,
            )
            place = lax.broadcasted_iota(jnp.int32, (ORDER - reached, ORDER), 1)
            in_panel = (place >= first) & (place < reached)
            work[reached:, :] = jnp.where(in_panel, 0.0, work[reached:, :]) - update


def finish_kernel(
    root_total,
    sums_ref,
    weighted,
    basis_hbm,
    factor_hbm,
    coef_hbm,
    work,
    upper,
    inverse,
    panel_rows,
    basis,
    coef,
    sems,
):
    count = coef.shape[0]
    work[0:HALF, :] = sums_ref[0:HALF, :]
    work[HALF:ORDER, HALF:ORDER] = sums_ref[HALF:ORDER, HALF:ORDER]
    work[HALF:ORDER, 0:HALF] = jnp.transpose(sums_ref[0:HALF, HALF:ORDER])
    eliminate(work, upper, inverse, panel_rows)
    copies = [pltpu.make_async_copy(upper, factor_hbm, sems.at[0])]
    copies[0].start()

    def apply(left):
        return lax.dot_general(
            left,
            inverse[...],
            (((1,), (1,)), ((), ())),
            precision=HIGHEST,
            preferred_element_type=F32,
        )

    cross = jnp.concatenate(
        [
            sums_ref[HALF : HALF + count, 0:HALF],
            sums_ref[HALF + count : HALF + 2 * count, 0:HALF],
        ],
        axis=1,
    )
    coef[...] = apply(cross) / F32(root_total)
    copies.append(pltpu.make_async_copy(coef, coef_hbm, sems.at[1]))
    copies[1].start()
    for part in range(basis.shape[0] // HALF):
        rows = slice(HALF * part, HALF * part + HALF)
        basis[rows, :] = apply(weighted[rows, :])
        copies.append(
            pltpu.make_async_copy(
                basis.at[rows, :], basis_hbm.at[rows, :], sems.at[2 + part]
            )
        )
        copies[-1].start()
    for copy in copies:
        copy.wait()


def per_device(snapshots, volumes, live_rows, probes):
    row_count = snapshots.shape[0]
    count = probes.shape[0]
    total_rows = row_count * CORES * PLANE * DEPTH
    in_vmem = pl.BlockSpec(memory_space=pltpu.VMEM)
    anywhere = pl.BlockSpec(memory_space=pl.ANY)
    volumes = volumes.reshape(1, row_count)
    dma = pltpu.SemaphoreType.DMA

    def reduce_body(*refs):
        reduce_kernel(total_rows, *refs)

    sums, weighted = pl.pallas_call(
        reduce_body,
        out_shape=(
            pltpu.VMEM((ORDER, ORDER), F32),
            pltpu.VMEM((row_count, ORDER), F32),
        ),
        in_specs=[pl.BlockSpec(memory_space=pltpu.HBM)] * 4,
        out_specs=(in_vmem, in_vmem),
        scratch_shapes=[
            pltpu.VMEM((row_count, ORDER), F32),
            pltpu.VMEM((1, row_count), F32),
            pltpu.SMEM((1,), jnp.int32),
            pltpu.VMEM((count, row_count), F32),
            pltpu.VMEM((ORDER, ORDER), F32),
            pltpu.VMEM((HALF, ORDER), F32),
            pltpu.VMEM((PLANE, TILE, ORDER), F32),
            pltpu.VMEM((DEPTH, TILE, ORDER), F32),
            pltpu.VMEM((ORDER, ORDER), F32),
            dma((4,)),
            pltpu.SemaphoreType.REGULAR((len(RELAYS),)),
            dma((2,)),
            dma((PLANE,)),
            dma((PLANE,)),
            dma((DEPTH,)),
            dma((DEPTH,)),
            dma((PLANE,)),
            dma((PLANE,)),
            dma((PLANE,)),
            dma((PLANE,)),
        ],
        compiler_params=pltpu.CompilerParams(collective_id=0, has_side_effects=True),
        name="reduce_sums",
    )(snapshots, volumes, live_rows, probes)

    def finish_body(*refs):
        finish_kernel(float(total_rows) ** 0.5, *refs)

    return pl.pallas_call(
        finish_body,
        out_shape=(
            jax.ShapeDtypeStruct((row_count, ORDER), F32),
            jax.ShapeDtypeStruct((ORDER, ORDER), F32),
            jax.ShapeDtypeStruct((count, ORDER), F32),
        ),
        in_specs=[in_vmem, in_vmem],
        out_specs=(anywhere, anywhere, anywhere),
        scratch_shapes=[
            pltpu.VMEM((ORDER, ORDER), F32),
            pltpu.VMEM((ORDER, ORDER), F32),
            pltpu.VMEM((ORDER, ORDER), F32),
            pltpu.VMEM((TILE * PANEL, ORDER), F32),
            pltpu.VMEM((row_count, ORDER), F32),
            pltpu.VMEM((count, ORDER), F32),
            dma((2 + row_count // HALF,)),
        ],
        name="factor_apply",
    )(
        pltpu.with_memory_space_constraint(sums, pltpu.VMEM),
        pltpu.with_memory_space_constraint(weighted, pltpu.VMEM),
    )


def solution(mesh):
    both = ("cells", "sub")
    placed = (P(both, None), P(both), P(both), P(None, both))
    return jax.shard_map(
        per_device,
        mesh=mesh,
        in_specs=placed,
        out_specs=(P(both, None), P(), P()),
        check_vma=False,
    )
```

```python
import jax
import jax.numpy as jnp
from jax import lax
from jax.experimental import pallas as pl
from jax.experimental.pallas import tpu as pltpu
from jax.sharding import PartitionSpec as P

HIGHEST = lax.Precision.HIGHEST
MESH = pl.DeviceIdType.MESH
F32 = jnp.float32

ORDER = 256
HALF = 128
TILE = 8
TILES = ORDER // TILE
PANEL = 8
AHEAD = 2
XS = 4
YS = 4
CORES = 2
PLANE = XS * YS
DEPTH = 16
RELAYS = (1, 2, 4)


def plane_offsets():
    places = [(dx, dy) for dx in range(XS) for dy in range(YS)]
    return sorted(places, key=hops, reverse=True)[:-1]


def hops(offset):
    return sum(min(d, size - d) for d, size in zip(offset, (XS, YS)))


def reduce_kernel(
    total_rows,
    snap_hbm,
    vol_hbm,
    live_hbm,
    probe_hbm,
    out_ref,
    weighted,
    snap,
    vol,
    live,
    probe,
    local,
    pair_buf,
    plane_buf,
    depth_buf,
    full,
    load_sems,
    relay_sems,
    pair_sems,
    plane_send,
    plane_recv,
    depth_send,
    depth_recv,
    full_send,
    full_recv,
    cross_send,
    cross_recv,
):
    cells = lax.axis_index("cells")
    sub = lax.axis_index("sub")
    z = cells // XS
    x = cells % XS
    y = sub // CORES
    core = sub % CORES
    me = x * YS + y

    def pair_id():
        return (cells, y * CORES + 1 - core)

    def plane_id(place):
        return (z * XS + place // YS, place % YS * CORES + core)

    def depth_id(place):
        return (place * XS + x, sub)

    targets = [(x + dx) % XS * YS + (y + dy) % YS for dx, dy in plane_offsets()]
    sources = [
        (x + XS - dx) % XS * YS + (y + YS - dy) % YS
        for dx, dy in reversed(plane_offsets())
    ]

    def signal(sem, device):
        pl.semaphore_signal(sem, inc=1, device_id=device, device_id_type=MESH)

    def relay(stage):
        for step in (RELAYS[stage], DEPTH - RELAYS[stage]):
            signal(relay_sems.at[stage], depth_id((z + step) % DEPTH))

    loads = [
        pltpu.make_async_copy(source, target, load_sems.at[i])
        for i, (source, target) in enumerate(
            [(live_hbm, live), (vol_hbm, vol), (snap_hbm, snap), (probe_hbm, probe)]
        )
    ]
    for load in loads:
        load.start()

    barrier = pltpu.get_barrier_semaphore()
    for other in targets:
        signal(barrier, plane_id(other))
    for step in (1, DEPTH - 1):
        signal(barrier, depth_id((z + step) % DEPTH))
    signal(barrier, pair_id())

    loads[0].wait()
    loads[1].wait()
    rows = vol.shape[1]
    slots = lax.broadcasted_iota(jnp.int32, (1, rows), 1)
    scale = jnp.where(slots < live[0], jnp.sqrt(vol[...]), 0.0)
    columns = jnp.transpose(jnp.broadcast_to(scale, (HALF, rows)))
    loads[2].wait()
    for half in range(2):
        part = slice(HALF * half, HALF * half + HALF)
        weighted[:, part] = snap[:, part] * columns

    def gram(left, right):
        return lax.dot_general(
            left,
            right,
            (((0,), (0,)), ((), ())),
            precision=HIGHEST,
            preferred_element_type=F32,
        ) * F32(1.0 / total_rows)

    local[0:HALF, :] = gram(weighted[:, 0:HALF], weighted[...])
    local[HALF:ORDER, HALF:ORDER] = gram(
        weighted[:, HALF:ORDER], weighted[:, HALF:ORDER]
    )
    loads[3].wait()
    cross = jnp.dot(
        probe[...] * scale, weighted[...], precision=HIGHEST, preferred_element_type=F32
    )
    count = cross.shape[0]
    local[HALF : HALF + count, 0:HALF] = cross[:, 0:HALF]
    local[HALF + count : HALF + 2 * count, 0:HALF] = cross[:, HALF:ORDER]

    pl.semaphore_wait(barrier, 1 + PLANE - 1 + 2)
    relay(0)

    def half_rows(which):
        return pl.ds(pl.multiple_of(which * HALF, HALF), HALF)

    pair = pltpu.make_async_remote_copy(
        src_ref=local.at[half_rows(1 - core), :],
        dst_ref=pair_buf,
        send_sem=pair_sems.at[0],
        recv_sem=pair_sems.at[1],
        device_id=pair_id(),
        device_id_type=MESH,
    )
    pair.start()
    pl.semaphore_wait(relay_sems.at[0], 2)
    relay(1)
    pair.wait()
    pair_buf[...] = pair_buf[...] + local[half_rows(core), :]

    def tile_of(place):
        return pl.ds(pl.multiple_of(place * TILE, TILE), TILE)

    def plane_copy(other):
        return pltpu.make_async_remote_copy(
            src_ref=pair_buf.at[tile_of(other), :],
            dst_ref=plane_buf.at[me],
            send_sem=plane_send.at[other],
            recv_sem=plane_recv.at[me],
            device_id=plane_id(other),
            device_id_type=MESH,
        )

    for other in targets:
        plane_copy(other).start()
    pl.semaphore_wait(relay_sems.at[1], 2)
    relay(2)
    total = pair_buf[tile_of(me), :]
    for other in sources:
        pltpu.make_async_copy(
            plane_buf.at[other], plane_buf.at[other], plane_recv.at[other]
        ).wait()
        total = total + plane_buf[other]

    depth_buf[z] = total

    def depth_copy(other):
        return pltpu.make_async_remote_copy(
            src_ref=depth_buf.at[z],
            dst_ref=depth_buf.at[z],
            send_sem=depth_send.at[other],
            recv_sem=depth_recv.at[z],
            device_id=depth_id(other),
            device_id_type=MESH,
        )

    def start_depth(step, carry):
        far = DEPTH // 2
        near = (step + 1) // 2 * (1 - step % 2 * 2)
        depth_copy((z + DEPTH + far - near) % DEPTH).start()
        return carry

    pl.semaphore_wait(relay_sems.at[2], 2)
    lax.fori_loop(0, DEPTH - 1, start_depth, 0)

    def wait_depth(step, carry):
        other = (z + step) % DEPTH
        pltpu.make_async_copy(
            depth_buf.at[other], depth_buf.at[other], depth_recv.at[other]
        ).wait()
        return carry

    lax.fori_loop(1, DEPTH, wait_depth, 0)
    summed = depth_buf[0]
    for place in range(1, DEPTH):
        summed = summed + depth_buf[place]

    def own_tile(place):
        return pl.ds(pl.multiple_of(core * HALF + place * TILE, TILE), TILE)

    full[own_tile(me), :] = summed

    def full_copy(other):
        return pltpu.make_async_remote_copy(
            src_ref=full.at[own_tile(me), :],
            dst_ref=full.at[own_tile(me), :],
            send_sem=full_send.at[other],
            recv_sem=full_recv.at[me],
            device_id=plane_id(other),
            device_id_type=MESH,
        )

    def other_core_copy(other):
        return pltpu.make_async_remote_copy(
            src_ref=full.at[own_tile(me), :],
            dst_ref=full.at[own_tile(me), :],
            send_sem=cross_send.at[other],
            recv_sem=cross_recv.at[me],
            device_id=(z * XS + other // YS, other % YS * CORES + 1 - core),
            device_id_type=MESH,
        )

    cross_pair = pltpu.make_async_remote_copy(
        src_ref=full.at[own_tile(me), :],
        dst_ref=full.at[own_tile(me), :],
        send_sem=cross_send.at[me],
        recv_sem=cross_recv.at[me],
        device_id=pair_id(),
        device_id_type=MESH,
    )
    for other in targets:
        full_copy(other).start()
        other_core_copy(other).start()
    cross_pair.start()

    def arrived(which, place, sems):
        tile = full.at[
            pl.ds(pl.multiple_of(which * HALF + place * TILE, TILE), TILE), :
        ]
        pltpu.make_async_copy(tile, tile, sems.at[place]).wait()

    arrived(1 - core, me, cross_recv)
    for other in sources:
        arrived(core, other, full_recv)
        arrived(1 - core, other, cross_recv)
    cross_pair.wait_send()

    def drain(step, carry):
        other = (me + step) % PLANE
        plane_copy(other).wait_send()
        full_copy(other).wait_send()
        other_core_copy(other).wait_send()
        return carry

    lax.fori_loop(1, PLANE, drain, 0)

    def drain_depth(step, carry):
        depth_copy((z + step) % DEPTH).wait_send()
        return carry

    lax.fori_loop(1, DEPTH, drain_depth, 0)

    out_ref[...] = full[...]


def lane_spread(block, lane):
    return jnp.broadcast_to(block[:, lane : lane + 1], (TILE, HALF))


def row_spread(block, row):
    return jnp.broadcast_to(block[row : row + 1, :], (TILE, HALF))


def stack_rows(row_in, rows):
    stacked = rows[0]
    for k in range(1, TILE):
        stacked = jnp.where(row_in == k, rows[k], stacked)
    return stacked


def eliminate(work, upper, lower_inverse, panel_rows):
    lane = lax.broadcasted_iota(jnp.int32, (TILE, HALF), 1)
    row_in = lax.broadcasted_iota(jnp.int32, (TILE, HALF), 0)
    for t in range(TILES):
        end = (t // PANEL + 1) * PANEL
        half, low = divmod(TILE * t, HALF)
        rows_t = slice(TILE * t, TILE * t + TILE)
        current = [work[rows_t, 0:HALF], work[rows_t, HALF:ORDER]]
        if t == 0:
            diag = [lane_spread(current[half], low + j) for j in range(TILE)]
        unit = jnp.where(lane == low + row_in, 1.0, 0.0)
        inside = (lane >= low) & (lane < low + TILE)
        last = t == TILES - 1
        if not last:
            rows_n = slice(TILE * t + TILE, TILE * t + 2 * TILE)
            after = [work[rows_n, 0:HALF], work[rows_n, HALF:ORDER]]
            half_n, low_n = divmod(TILE * t + TILE, HALF)
            diag_n = [lane_spread(after[half_n], low_n + j) for j in range(TILE)]
            below = [lane_spread(after[half], low + j) for j in range(TILE)]
        pivots, unit_pivots, factors = [], [], []
        for k in range(TILE):
            root = lax.rsqrt(row_spread(diag[k], k))
            column = diag[k] * root
            masked = jnp.where(row_in > k, column, 0.0)
            entries = {j: row_spread(column, j) for j in range(k + 1, TILE)}
            for j in range(k + 1, TILE):
                diag[j] = diag[j] - column * entries[j]
            pivot = [row_spread(current[i], k) * root for i in range(2)]
            unit_pivot = row_spread(unit, k) * root
            if k < TILE - 1:
                current = [current[i] - masked * pivot[i] for i in range(2)]
                unit = unit - masked * unit_pivot
            pivots.append(pivot)
            unit_pivots.append(unit_pivot)
            if not last:
                factor = below[k] * root
                for j in range(k + 1, TILE):
                    below[j] = below[j] - factor * entries[j]
                for j in range(TILE):
                    diag_n[j] = diag_n[j] - factor * row_spread(factor, j)
                factors.append(factor)
        own = stack_rows(row_in, [pivots[k][half] for k in range(TILE)])
        for k in range(TILE):
            pivots[k][half] = jnp.where(inside, unit_pivots[k], pivots[k][half])
        done = [
            stack_rows(row_in, [pivots[k][i] for k in range(TILE)]) for i in range(2)
        ]
        for i in range(2):
            columns = slice(HALF * i, HALF * i + HALF)
            place = lane + HALF * i
            lower_inverse[rows_t, columns] = jnp.where(
                place < TILE * t + TILE, done[i], 0.0
            )
            shown = jnp.where(inside, own, done[i]) if i == half else done[i]
            upper[rows_t, columns] = jnp.where(place >= TILE * t + row_in, shown, 0.0)
            panel_rows[TILE * (t % PANEL) : TILE * (t % PANEL) + TILE, columns] = (
                jnp.where(
                    (place >= TILE * t + TILE) & (place < TILE * end), 0.0, done[i]
                )
            )
        if not last:
            after[half] = jnp.where(inside, 0.0, after[half])
            for k in range(TILE):
                after = [after[i] - factors[k] * pivots[k][i] for i in range(2)]
            work[rows_n, 0:HALF] = after[0]
            work[rows_n, HALF:ORDER] = after[1]
            diag = diag_n
            stop = min(end + AHEAD, TILES)
            rest = range(t + 2, stop)
            if len(rest) > 0:
                halves = range((TILE * t + 2 * TILE) // HALF, (TILE * stop - 1) // HALF + 1)
                turned = {i: jnp.transpose(done[i]) for i in halves}
                tiles = {}
                for s in rest:
                    rows_s = slice(TILE * s, TILE * s + TILE)
                    tiles[s] = [work[rows_s, 0:HALF], work[rows_s, HALF:ORDER]]
                    tiles[s][half] = jnp.where(inside, 0.0, tiles[s][half])
                for k in range(TILE):
                    for s in rest:
                        i_s, low_s = divmod(TILE * s, HALF)
                        spread = lane_spread(turned[i_s][low_s : low_s + TILE, :], k)
                        tiles[s] = [
                            tiles[s][i] - spread * pivots[k][i] for i in range(2)
                        ]
                for s in rest:
                    rows_s = slice(TILE * s, TILE * s + TILE)
                    work[rows_s, 0:HALF] = tiles[s][0]
                    work[rows_s, HALF:ORDER] = tiles[s][1]
        if t == end - 1 and end + AHEAD < TILES:
            reached = TILE * (end + AHEAD)
            first = TILE * (end - PANEL)
            turned = jnp.transpose(panel_rows[...])
            update = jnp.dot(
                turned[reached:, :],
                panel_rows[...],
                precision=HIGHEST,
                preferred_element_type=F32,
            )
            place = lax.broadcasted_iota(jnp.int32, (ORDER - reached, ORDER), 1)
            in_panel = (place >= first) & (place < TILE * end)
            work[reached:, :] = jnp.where(in_panel, 0.0, work[reached:, :]) - update


def finish_kernel(
    root_total,
    sums_ref,
    weighted,
    basis_hbm,
    factor_hbm,
    coef_hbm,
    work,
    upper,
    inverse,
    panel_rows,
    basis,
    coef,
    sems,
):
    count = coef.shape[0]
    work[0:HALF, :] = sums_ref[0:HALF, :]
    work[HALF:ORDER, HALF:ORDER] = sums_ref[HALF:ORDER, HALF:ORDER]
    work[HALF:ORDER, 0:HALF] = jnp.transpose(sums_ref[0:HALF, HALF:ORDER])
    eliminate(work, upper, inverse, panel_rows)
    copies = [pltpu.make_async_copy(upper, factor_hbm, sems.at[0])]
    copies[0].start()

    def apply(left):
        return lax.dot_general(
            left,
            inverse[...],
            (((1,), (1,)), ((), ())),
            precision=HIGHEST,
            preferred_element_type=F32,
        )

    cross = jnp.concatenate(
        [
            sums_ref[HALF : HALF + count, 0:HALF],
            sums_ref[HALF + count : HALF + 2 * count, 0:HALF],
        ],
        axis=1,
    )
    coef[...] = apply(cross) / F32(root_total)
    copies.append(pltpu.make_async_copy(coef, coef_hbm, sems.at[1]))
    copies[1].start()
    for part in range(basis.shape[0] // HALF):
        rows = slice(HALF * part, HALF * part + HALF)
        basis[rows, :] = apply(weighted[rows, :])
        copies.append(
            pltpu.make_async_copy(
                basis.at[rows, :], basis_hbm.at[rows, :], sems.at[2 + part]
            )
        )
        copies[-1].start()
    for copy in copies:
        copy.wait()


def per_device(snapshots, volumes, live_rows, probes):
    row_count = snapshots.shape[0]
    count = probes.shape[0]
    total_rows = row_count * CORES * PLANE * DEPTH
    in_vmem = pl.BlockSpec(memory_space=pltpu.VMEM)
    anywhere = pl.BlockSpec(memory_space=pl.ANY)
    volumes = volumes.reshape(1, row_count)
    dma = pltpu.SemaphoreType.DMA

    def reduce_body(*refs):
        reduce_kernel(total_rows, *refs)

    sums, weighted = pl.pallas_call(
        reduce_body,
        out_shape=(
            pltpu.VMEM((ORDER, ORDER), F32),
            pltpu.VMEM((row_count, ORDER), F32),
        ),
        in_specs=[pl.BlockSpec(memory_space=pltpu.HBM)] * 4,
        out_specs=(in_vmem, in_vmem),
        scratch_shapes=[
            pltpu.VMEM((row_count, ORDER), F32),
            pltpu.VMEM((1, row_count), F32),
            pltpu.SMEM((1,), jnp.int32),
            pltpu.VMEM((count, row_count), F32),
            pltpu.VMEM((ORDER, ORDER), F32),
            pltpu.VMEM((HALF, ORDER), F32),
            pltpu.VMEM((PLANE, TILE, ORDER), F32),
            pltpu.VMEM((DEPTH, TILE, ORDER), F32),
            pltpu.VMEM((ORDER, ORDER), F32),
            dma((4,)),
            pltpu.SemaphoreType.REGULAR((len(RELAYS),)),
            dma((2,)),
            dma((PLANE,)),
            dma((PLANE,)),
            dma((DEPTH,)),
            dma((DEPTH,)),
            dma((PLANE,)),
            dma((PLANE,)),
            dma((PLANE,)),
            dma((PLANE,)),
        ],
        compiler_params=pltpu.CompilerParams(collective_id=0, has_side_effects=True),
        name="reduce_sums",
    )(snapshots, volumes, live_rows, probes)

    def finish_body(*refs):
        finish_kernel(float(total_rows) ** 0.5, *refs)

    return pl.pallas_call(
        finish_body,
        out_shape=(
            jax.ShapeDtypeStruct((row_count, ORDER), F32),
            jax.ShapeDtypeStruct((ORDER, ORDER), F32),
            jax.ShapeDtypeStruct((count, ORDER), F32),
        ),
        in_specs=[in_vmem, in_vmem],
        out_specs=(anywhere, anywhere, anywhere),
        scratch_shapes=[
            pltpu.VMEM((ORDER, ORDER), F32),
            pltpu.VMEM((ORDER, ORDER), F32),
            pltpu.VMEM((ORDER, ORDER), F32),
            pltpu.VMEM((TILE * PANEL, ORDER), F32),
            pltpu.VMEM((row_count, ORDER), F32),
            pltpu.VMEM((count, ORDER), F32),
            dma((2 + row_count // HALF,)),
        ],
        name="factor_apply",
    )(
        pltpu.with_memory_space_constraint(sums, pltpu.VMEM),
        pltpu.with_memory_space_constraint(weighted, pltpu.VMEM),
    )


def solution(mesh):
    both = ("cells", "sub")
    placed = (P(both, None), P(both), P(both), P(None, both))
    return jax.shard_map(
        per_device,
        mesh=mesh,
        in_specs=placed,
        out_specs=(P(both, None), P(), P()),
        check_vma=False,
    )
```

```python
import jax
import jax.numpy as jnp
from jax import lax
from jax.experimental import pallas as pl
from jax.experimental.pallas import tpu as pltpu
from jax.sharding import PartitionSpec as P

HIGHEST = lax.Precision.HIGHEST
MESH = pl.DeviceIdType.MESH
F32 = jnp.float32

ORDER = 256
HALF = 128
TILE = 8
TILES = ORDER // TILE
PANEL = 8
AHEAD = 2
XS = 4
YS = 4
CORES = 2
PLANE = XS * YS
DEPTH = 16
RELAYS = (1, 2, 4)


def plane_offsets():
    places = [(dx, dy) for dx in range(XS) for dy in range(YS)]
    return sorted(places, key=hops, reverse=True)[:-1]


def hops(offset):
    return sum(min(d, size - d) for d, size in zip(offset, (XS, YS)))


def reduce_kernel(
    total_rows,
    snap_hbm,
    vol_hbm,
    live_hbm,
    probe_hbm,
    out_ref,
    weighted,
    snap,
    vol,
    live,
    probe,
    local,
    pair_buf,
    plane_buf,
    depth_buf,
    full,
    load_sems,
    relay_sems,
    pair_sems,
    send_sems,
    recv_sems,
):
    cells = lax.axis_index("cells")
    sub = lax.axis_index("sub")
    z = cells // XS
    x = cells % XS
    y = sub // CORES
    core = sub % CORES
    me = x * YS + y

    def pair_id():
        return (cells, y * CORES + 1 - core)

    def plane_id(place):
        return (z * XS + place // YS, place % YS * CORES + core)

    def depth_id(place):
        return (place * XS + x, sub)

    targets = [(x + dx) % XS * YS + (y + dy) % YS for dx, dy in plane_offsets()]
    sources = [
        (x + XS - dx) % XS * YS + (y + YS - dy) % YS
        for dx, dy in reversed(plane_offsets())
    ]

    def settle(sem, tiles):
        part = full.at[pl.ds(0, tiles * TILE), :]
        pltpu.make_async_copy(part, part, sem).wait()

    def signal(sem, device):
        pl.semaphore_signal(sem, inc=1, device_id=device, device_id_type=MESH)

    def relay(stage):
        for step in (RELAYS[stage], DEPTH - RELAYS[stage]):
            signal(relay_sems.at[stage], depth_id((z + step) % DEPTH))

    loads = [
        pltpu.make_async_copy(source, target, load_sems.at[i])
        for i, (source, target) in enumerate(
            [(live_hbm, live), (vol_hbm, vol), (snap_hbm, snap), (probe_hbm, probe)]
        )
    ]
    for load in loads:
        load.start()

    barrier = pltpu.get_barrier_semaphore()
    for other in targets:
        signal(barrier, plane_id(other))
    for step in (1, DEPTH - 1):
        signal(barrier, depth_id((z + step) % DEPTH))
    signal(barrier, pair_id())

    loads[0].wait()
    loads[1].wait()
    rows = vol.shape[1]
    slots = lax.broadcasted_iota(jnp.int32, (1, rows), 1)
    scale = jnp.where(slots < live[0], jnp.sqrt(vol[...]), 0.0)
    columns = jnp.transpose(jnp.broadcast_to(scale, (HALF, rows)))
    loads[2].wait()
    for half in range(2):
        part = slice(HALF * half, HALF * half + HALF)
        weighted[:, part] = snap[:, part] * columns

    def gram(left, right):
        return lax.dot_general(
            left,
            right,
            (((0,), (0,)), ((), ())),
            precision=HIGHEST,
            preferred_element_type=F32,
        ) * F32(1.0 / total_rows)

    local[0:HALF, :] = gram(weighted[:, 0:HALF], weighted[...])
    local[HALF:ORDER, HALF:ORDER] = gram(
        weighted[:, HALF:ORDER], weighted[:, HALF:ORDER]
    )
    loads[3].wait()
    cross = jnp.dot(
        probe[...] * scale, weighted[...], precision=HIGHEST, preferred_element_type=F32
    )
    count = cross.shape[0]
    local[HALF : HALF + count, 0:HALF] = cross[:, 0:HALF]
    local[HALF + count : HALF + 2 * count, 0:HALF] = cross[:, HALF:ORDER]

    pl.semaphore_wait(barrier, 1 + PLANE - 1 + 2)
    relay(0)

    def half_rows(which):
        return pl.ds(pl.multiple_of(which * HALF, HALF), HALF)

    pair = pltpu.make_async_remote_copy(
        src_ref=local.at[half_rows(1 - core), :],
        dst_ref=pair_buf,
        send_sem=pair_sems.at[0],
        recv_sem=pair_sems.at[1],
        device_id=pair_id(),
        device_id_type=MESH,
    )
    pair.start()
    pl.semaphore_wait(relay_sems.at[0], 2)
    relay(1)
    pair.wait()
    pair_buf[...] = pair_buf[...] + local[half_rows(core), :]

    def tile_of(place):
        return pl.ds(pl.multiple_of(place * TILE, TILE), TILE)

    def plane_copy(other):
        return pltpu.make_async_remote_copy(
            src_ref=pair_buf.at[tile_of(other), :],
            dst_ref=plane_buf.at[me],
            send_sem=send_sems.at[0],
            recv_sem=recv_sems.at[0],
            device_id=plane_id(other),
            device_id_type=MESH,
        )

    for other in targets:
        plane_copy(other).start()
    pl.semaphore_wait(relay_sems.at[1], 2)
    relay(2)
    settle(recv_sems.at[0], PLANE - 1)
    total = pair_buf[tile_of(me), :]
    for other in sources:
        total = total + plane_buf[other]

    depth_buf[z] = total

    def depth_copy(other):
        return pltpu.make_async_remote_copy(
            src_ref=depth_buf.at[z],
            dst_ref=depth_buf.at[z],
            send_sem=send_sems.at[1],
            recv_sem=recv_sems.at[1],
            device_id=depth_id(other),
            device_id_type=MESH,
        )

    pl.semaphore_wait(relay_sems.at[2], 2)
    for step in range(DEPTH // 2, 0, -1):
        depth_copy((z + step) % DEPTH).start()
        if step < DEPTH // 2:
            depth_copy((z + DEPTH - step) % DEPTH).start()
    settle(send_sems.at[0], PLANE - 1)
    settle(recv_sems.at[1], DEPTH - 1)
    summed = depth_buf[0]
    for place in range(1, DEPTH):
        summed = summed + depth_buf[place]

    def own_tile(place):
        return pl.ds(pl.multiple_of(core * HALF + place * TILE, TILE), TILE)

    full[own_tile(me), :] = summed

    def full_copy(place, which):
        return pltpu.make_async_remote_copy(
            src_ref=full.at[own_tile(me), :],
            dst_ref=full.at[own_tile(me), :],
            send_sem=send_sems.at[2],
            recv_sem=recv_sems.at[2],
            device_id=(z * XS + place // YS, place % YS * CORES + which),
            device_id_type=MESH,
        )

    for other in targets:
        full_copy(other, core).start()
        full_copy(other, 1 - core).start()
    full_copy(me, 1 - core).start()
    settle(send_sems.at[1], DEPTH - 1)
    settle(recv_sems.at[2], CORES * PLANE - 1)
    settle(send_sems.at[2], CORES * PLANE - 1)
    out_ref[...] = full[...]


def lane_spread(block, lane):
    return jnp.broadcast_to(block[:, lane : lane + 1], (TILE, HALF))


def row_spread(block, row):
    return jnp.broadcast_to(block[row : row + 1, :], (TILE, HALF))


def stack_rows(row_in, rows):
    stacked = rows[0]
    for k in range(1, TILE):
        stacked = jnp.where(row_in == k, rows[k], stacked)
    return stacked


def eliminate(work, upper, lower_inverse, panel_rows):
    lane = lax.broadcasted_iota(jnp.int32, (TILE, HALF), 1)
    row_in = lax.broadcasted_iota(jnp.int32, (TILE, HALF), 0)
    for t in range(TILES):
        end = (t // PANEL + 1) * PANEL
        half, low = divmod(TILE * t, HALF)
        rows_t = slice(TILE * t, TILE * t + TILE)
        current = [work[rows_t, 0:HALF], work[rows_t, HALF:ORDER]]
        if t == 0:
            diag = [lane_spread(current[half], low + j) for j in range(TILE)]
        unit = jnp.where(lane == low + row_in, 1.0, 0.0)
        inside = (lane >= low) & (lane < low + TILE)
        last = t == TILES - 1
        if not last:
            rows_n = slice(TILE * t + TILE, TILE * t + 2 * TILE)
            after = [work[rows_n, 0:HALF], work[rows_n, HALF:ORDER]]
            half_n, low_n = divmod(TILE * t + TILE, HALF)
            diag_n = [lane_spread(after[half_n], low_n + j) for j in range(TILE)]
            below = [lane_spread(after[half], low + j) for j in range(TILE)]
        pivots, unit_pivots, factors = [], [], []
        for k in range(TILE):
            root = lax.rsqrt(row_spread(diag[k], k))
            column = diag[k] * root
            masked = jnp.where(row_in > k, column, 0.0)
            entries = {j: row_spread(column, j) for j in range(k + 1, TILE)}
            for j in range(k + 1, TILE):
                diag[j] = diag[j] - column * entries[j]
            pivot = [row_spread(current[i], k) * root for i in range(2)]
            unit_pivot = row_spread(unit, k) * root
            if k < TILE - 1:
                current = [current[i] - masked * pivot[i] for i in range(2)]
                unit = unit - masked * unit_pivot
            pivots.append(pivot)
            unit_pivots.append(unit_pivot)
            if not last:
                factor = below[k] * root
                for j in range(k + 1, TILE):
                    below[j] = below[j] - factor * entries[j]
                for j in range(TILE):
                    diag_n[j] = diag_n[j] - factor * row_spread(factor, j)
                factors.append(factor)
        own = stack_rows(row_in, [pivots[k][half] for k in range(TILE)])
        for k in range(TILE):
            pivots[k][half] = jnp.where(inside, unit_pivots[k], pivots[k][half])
        done = [
            stack_rows(row_in, [pivots[k][i] for k in range(TILE)]) for i in range(2)
        ]
        for i in range(2):
            columns = slice(HALF * i, HALF * i + HALF)
            place = lane + HALF * i
            lower_inverse[rows_t, columns] = jnp.where(
                place < TILE * t + TILE, done[i], 0.0
            )
            shown = jnp.where(inside, own, done[i]) if i == half else done[i]
            upper[rows_t, columns] = jnp.where(place >= TILE * t + row_in, shown, 0.0)
            panel_rows[TILE * (t % PANEL) : TILE * (t % PANEL) + TILE, columns] = (
                jnp.where(
                    (place >= TILE * t + TILE) & (place < TILE * end), 0.0, done[i]
                )
            )
        if not last:
            after[half] = jnp.where(inside, 0.0, after[half])
            for k in range(TILE):
                after = [after[i] - factors[k] * pivots[k][i] for i in range(2)]
            work[rows_n, 0:HALF] = after[0]
            work[rows_n, HALF:ORDER] = after[1]
            diag = diag_n
            stop = min(end + AHEAD, TILES)
            rest = range(t + 2, stop)
            if len(rest) > 0:
                halves = range((TILE * t + 2 * TILE) // HALF, (TILE * stop - 1) // HALF + 1)
                turned = {i: jnp.transpose(done[i]) for i in halves}
                tiles = {}
                for s in rest:
                    rows_s = slice(TILE * s, TILE * s + TILE)
                    tiles[s] = [work[rows_s, 0:HALF], work[rows_s, HALF:ORDER]]
                    tiles[s][half] = jnp.where(inside, 0.0, tiles[s][half])
                for k in range(TILE):
                    for s in rest:
                        i_s, low_s = divmod(TILE * s, HALF)
                        spread = lane_spread(turned[i_s][low_s : low_s + TILE, :], k)
                        tiles[s] = [
                            tiles[s][i] - spread * pivots[k][i] for i in range(2)
                        ]
                for s in rest:
                    rows_s = slice(TILE * s, TILE * s + TILE)
                    work[rows_s, 0:HALF] = tiles[s][0]
                    work[rows_s, HALF:ORDER] = tiles[s][1]
        if t == end - 1 and end + AHEAD < TILES:
            reached = TILE * (end + AHEAD)
            first = TILE * (end - PANEL)
            turned = jnp.transpose(panel_rows[...])
            update = jnp.dot(
                turned[reached:, :],
                panel_rows[...],
                precision=HIGHEST,
                preferred_element_type=F32,
            )
            place = lax.broadcasted_iota(jnp.int32, (ORDER - reached, ORDER), 1)
            in_panel = (place >= first) & (place < TILE * end)
            work[reached:, :] = jnp.where(in_panel, 0.0, work[reached:, :]) - update


def finish_kernel(
    root_total,
    sums_ref,
    weighted,
    basis_hbm,
    factor_hbm,
    coef_hbm,
    work,
    upper,
    inverse,
    panel_rows,
    basis,
    coef,
    sems,
):
    count = coef.shape[0]
    work[0:HALF, :] = sums_ref[0:HALF, :]
    work[HALF:ORDER, HALF:ORDER] = sums_ref[HALF:ORDER, HALF:ORDER]
    work[HALF:ORDER, 0:HALF] = jnp.transpose(sums_ref[0:HALF, HALF:ORDER])
    eliminate(work, upper, inverse, panel_rows)
    copies = [pltpu.make_async_copy(upper, factor_hbm, sems.at[0])]
    copies[0].start()

    def apply(left):
        return lax.dot_general(
            left,
            inverse[...],
            (((1,), (1,)), ((), ())),
            precision=HIGHEST,
            preferred_element_type=F32,
        )

    cross = jnp.concatenate(
        [
            sums_ref[HALF : HALF + count, 0:HALF],
            sums_ref[HALF + count : HALF + 2 * count, 0:HALF],
        ],
        axis=1,
    )
    coef[...] = apply(cross) / F32(root_total)
    copies.append(pltpu.make_async_copy(coef, coef_hbm, sems.at[1]))
    copies[1].start()
    for part in range(basis.shape[0] // HALF):
        rows = slice(HALF * part, HALF * part + HALF)
        basis[rows, :] = apply(weighted[rows, :])
        copies.append(
            pltpu.make_async_copy(
                basis.at[rows, :], basis_hbm.at[rows, :], sems.at[2 + part]
            )
        )
        copies[-1].start()
    for copy in copies:
        copy.wait()


def per_device(snapshots, volumes, live_rows, probes):
    row_count = snapshots.shape[0]
    count = probes.shape[0]
    total_rows = row_count * CORES * PLANE * DEPTH
    in_vmem = pl.BlockSpec(memory_space=pltpu.VMEM)
    anywhere = pl.BlockSpec(memory_space=pl.ANY)
    volumes = volumes.reshape(1, row_count)
    dma = pltpu.SemaphoreType.DMA

    def reduce_body(*refs):
        reduce_kernel(total_rows, *refs)

    sums, weighted = pl.pallas_call(
        reduce_body,
        out_shape=(
            pltpu.VMEM((ORDER, ORDER), F32),
            pltpu.VMEM((row_count, ORDER), F32),
        ),
        in_specs=[pl.BlockSpec(memory_space=pltpu.HBM)] * 4,
        out_specs=(in_vmem, in_vmem),
        scratch_shapes=[
            pltpu.VMEM((row_count, ORDER), F32),
            pltpu.VMEM((1, row_count), F32),
            pltpu.SMEM((1,), jnp.int32),
            pltpu.VMEM((count, row_count), F32),
            pltpu.VMEM((ORDER, ORDER), F32),
            pltpu.VMEM((HALF, ORDER), F32),
            pltpu.VMEM((PLANE, TILE, ORDER), F32),
            pltpu.VMEM((DEPTH, TILE, ORDER), F32),
            pltpu.VMEM((ORDER, ORDER), F32),
            dma((4,)),
            pltpu.SemaphoreType.REGULAR((len(RELAYS),)),
            dma((2,)),
            dma((3,)),
            dma((3,)),
        ],
        compiler_params=pltpu.CompilerParams(collective_id=0, has_side_effects=True),
        name="reduce_sums",
    )(snapshots, volumes, live_rows, probes)

    def finish_body(*refs):
        finish_kernel(float(total_rows) ** 0.5, *refs)

    return pl.pallas_call(
        finish_body,
        out_shape=(
            jax.ShapeDtypeStruct((row_count, ORDER), F32),
            jax.ShapeDtypeStruct((ORDER, ORDER), F32),
            jax.ShapeDtypeStruct((count, ORDER), F32),
        ),
        in_specs=[in_vmem, in_vmem],
        out_specs=(anywhere, anywhere, anywhere),
        scratch_shapes=[
            pltpu.VMEM((ORDER, ORDER), F32),
            pltpu.VMEM((ORDER, ORDER), F32),
            pltpu.VMEM((ORDER, ORDER), F32),
            pltpu.VMEM((TILE * PANEL, ORDER), F32),
            pltpu.VMEM((row_count, ORDER), F32),
            pltpu.VMEM((count, ORDER), F32),
            dma((2 + row_count // HALF,)),
        ],
        name="factor_apply",
    )(
        pltpu.with_memory_space_constraint(sums, pltpu.VMEM),
        pltpu.with_memory_space_constraint(weighted, pltpu.VMEM),
    )


def solution(mesh):
    both = ("cells", "sub")
    placed = (P(both, None), P(both), P(both), P(None, both))
    return jax.shard_map(
        per_device,
        mesh=mesh,
        in_specs=placed,
        out_specs=(P(both, None), P(), P()),
        check_vma=False,
    )
```

```python
import jax
import jax.numpy as jnp
from jax import lax
from jax.experimental import pallas as pl
from jax.experimental.pallas import tpu as pltpu
from jax.sharding import PartitionSpec as P

HIGHEST = lax.Precision.HIGHEST
MESH = pl.DeviceIdType.MESH
F32 = jnp.float32

ORDER = 256
HALF = 128
TILE = 8
TILES = ORDER // TILE
PANEL = 8
AHEAD = 3
XS = 4
YS = 4
CORES = 2
PLANE = XS * YS
DEPTH = 16
RELAYS = (1, 2, 4)


def plane_offsets():
    places = [(dx, dy) for dx in range(XS) for dy in range(YS)]
    return sorted(places, key=hops, reverse=True)[:-1]


def hops(offset):
    return sum(min(d, size - d) for d, size in zip(offset, (XS, YS)))


def reduce_kernel(
    total_rows,
    snap_hbm,
    vol_hbm,
    live_hbm,
    probe_hbm,
    out_ref,
    weighted,
    snap,
    vol,
    live,
    probe,
    local,
    pair_buf,
    plane_buf,
    depth_buf,
    full,
    load_sems,
    relay_sems,
    pair_sems,
    send_sems,
    recv_sems,
):
    cells = lax.axis_index("cells")
    sub = lax.axis_index("sub")
    z = cells // XS
    x = cells % XS
    y = sub // CORES
    core = sub % CORES
    me = x * YS + y

    def pair_id():
        return (cells, y * CORES + 1 - core)

    def plane_id(place):
        return (z * XS + place // YS, place % YS * CORES + core)

    def depth_id(place):
        return (place * XS + x, sub)

    targets = [(x + dx) % XS * YS + (y + dy) % YS for dx, dy in plane_offsets()]
    sources = [
        (x + XS - dx) % XS * YS + (y + YS - dy) % YS
        for dx, dy in reversed(plane_offsets())
    ]

    def settle(sem, tiles):
        part = full.at[pl.ds(0, tiles * TILE), :]
        pltpu.make_async_copy(part, part, sem).wait()

    def signal(sem, device):
        pl.semaphore_signal(sem, inc=1, device_id=device, device_id_type=MESH)

    def relay(stage):
        for step in (RELAYS[stage], DEPTH - RELAYS[stage]):
            signal(relay_sems.at[stage], depth_id((z + step) % DEPTH))

    loads = [
        pltpu.make_async_copy(source, target, load_sems.at[i])
        for i, (source, target) in enumerate(
            [(live_hbm, live), (vol_hbm, vol), (snap_hbm, snap), (probe_hbm, probe)]
        )
    ]
    for load in loads:
        load.start()

    barrier = pltpu.get_barrier_semaphore()
    for other in targets:
        signal(barrier, plane_id(other))
    for step in (1, DEPTH - 1):
        signal(barrier, depth_id((z + step) % DEPTH))
    signal(barrier, pair_id())

    loads[0].wait()
    loads[1].wait()
    rows = vol.shape[1]
    slots = lax.broadcasted_iota(jnp.int32, (1, rows), 1)
    scale = jnp.where(slots < live[0], jnp.sqrt(vol[...]), 0.0)
    columns = jnp.transpose(jnp.broadcast_to(scale, (HALF, rows)))
    loads[2].wait()
    for half in range(2):
        part = slice(HALF * half, HALF * half + HALF)
        weighted[:, part] = snap[:, part] * columns

    def gram(left, right):
        return lax.dot_general(
            left,
            right,
            (((0,), (0,)), ((), ())),
            precision=HIGHEST,
            preferred_element_type=F32,
        ) * F32(1.0 / total_rows)

    local[0:HALF, :] = gram(weighted[:, 0:HALF], weighted[...])
    local[HALF:ORDER, HALF:ORDER] = gram(
        weighted[:, HALF:ORDER], weighted[:, HALF:ORDER]
    )
    loads[3].wait()
    cross = jnp.dot(
        probe[...] * scale, weighted[...], precision=HIGHEST, preferred_element_type=F32
    )
    count = cross.shape[0]
    local[HALF : HALF + count, 0:HALF] = cross[:, 0:HALF]
    local[HALF + count : HALF + 2 * count, 0:HALF] = cross[:, HALF:ORDER]

    pl.semaphore_wait(barrier, 1 + PLANE - 1 + 2)
    relay(0)

    def half_rows(which):
        return pl.ds(pl.multiple_of(which * HALF, HALF), HALF)

    pair = pltpu.make_async_remote_copy(
        src_ref=local.at[half_rows(1 - core), :],
        dst_ref=pair_buf,
        send_sem=pair_sems.at[0],
        recv_sem=pair_sems.at[1],
        device_id=pair_id(),
        device_id_type=MESH,
    )
    pair.start()
    pl.semaphore_wait(relay_sems.at[0], 2)
    relay(1)
    pair.wait()
    pair_buf[...] = pair_buf[...] + local[half_rows(core), :]

    def tile_of(place):
        return pl.ds(pl.multiple_of(place * TILE, TILE), TILE)

    def plane_copy(other):
        return pltpu.make_async_remote_copy(
            src_ref=pair_buf.at[tile_of(other), :],
            dst_ref=plane_buf.at[me],
            send_sem=send_sems.at[0],
            recv_sem=recv_sems.at[0],
            device_id=plane_id(other),
            device_id_type=MESH,
        )

    for other in targets:
        plane_copy(other).start()
    pl.semaphore_wait(relay_sems.at[1], 2)
    relay(2)
    settle(recv_sems.at[0], PLANE - 1)
    total = pair_buf[tile_of(me), :]
    for other in sources:
        total = total + plane_buf[other]

    depth_buf[z] = total

    def depth_copy(other):
        return pltpu.make_async_remote_copy(
            src_ref=depth_buf.at[z],
            dst_ref=depth_buf.at[z],
            send_sem=send_sems.at[1],
            recv_sem=recv_sems.at[1],
            device_id=depth_id(other),
            device_id_type=MESH,
        )

    pl.semaphore_wait(relay_sems.at[2], 2)
    for step in range(DEPTH // 2, 0, -1):
        depth_copy((z + step) % DEPTH).start()
        if step < DEPTH // 2:
            depth_copy((z + DEPTH - step) % DEPTH).start()
    settle(send_sems.at[0], PLANE - 1)
    settle(recv_sems.at[1], DEPTH - 1)
    summed = depth_buf[0]
    for place in range(1, DEPTH):
        summed = summed + depth_buf[place]

    def own_tile(place):
        return pl.ds(pl.multiple_of(core * HALF + place * TILE, TILE), TILE)

    full[own_tile(me), :] = summed

    def full_copy(place, which):
        return pltpu.make_async_remote_copy(
            src_ref=full.at[own_tile(me), :],
            dst_ref=full.at[own_tile(me), :],
            send_sem=send_sems.at[2],
            recv_sem=recv_sems.at[2],
            device_id=(z * XS + place // YS, place % YS * CORES + which),
            device_id_type=MESH,
        )

    for other in targets:
        full_copy(other, core).start()
        full_copy(other, 1 - core).start()
    full_copy(me, 1 - core).start()
    settle(send_sems.at[1], DEPTH - 1)
    settle(recv_sems.at[2], CORES * PLANE - 1)
    settle(send_sems.at[2], CORES * PLANE - 1)
    out_ref[...] = full[...]


def lane_spread(block, lane):
    return jnp.broadcast_to(block[:, lane : lane + 1], (TILE, HALF))


def row_spread(block, row):
    return jnp.broadcast_to(block[row : row + 1, :], (TILE, HALF))


def stack_rows(row_in, rows):
    stacked = rows[0]
    for k in range(1, TILE):
        stacked = jnp.where(row_in == k, rows[k], stacked)
    return stacked


def eliminate(work, upper, lower_inverse, panel_rows):
    lane = lax.broadcasted_iota(jnp.int32, (TILE, HALF), 1)
    row_in = lax.broadcasted_iota(jnp.int32, (TILE, HALF), 0)
    for t in range(TILES):
        end = (t // PANEL + 1) * PANEL
        half, low = divmod(TILE * t, HALF)
        rows_t = slice(TILE * t, TILE * t + TILE)
        current = [work[rows_t, 0:HALF], work[rows_t, HALF:ORDER]]
        if t == 0:
            diag = [lane_spread(current[half], low + j) for j in range(TILE)]
        unit = jnp.where(lane == low + row_in, 1.0, 0.0)
        inside = (lane >= low) & (lane < low + TILE)
        last = t == TILES - 1
        if not last:
            rows_n = slice(TILE * t + TILE, TILE * t + 2 * TILE)
            after = [work[rows_n, 0:HALF], work[rows_n, HALF:ORDER]]
            half_n, low_n = divmod(TILE * t + TILE, HALF)
            diag_n = [lane_spread(after[half_n], low_n + j) for j in range(TILE)]
            below = [lane_spread(after[half], low + j) for j in range(TILE)]
        pivots, unit_pivots, factors = [], [], []
        for k in range(TILE):
            root = lax.rsqrt(row_spread(diag[k], k))
            column = diag[k] * root
            masked = jnp.where(row_in > k, column, 0.0)
            entries = {j: row_spread(column, j) for j in range(k + 1, TILE)}
            for j in range(k + 1, TILE):
                diag[j] = diag[j] - column * entries[j]
            pivot = [row_spread(current[i], k) * root for i in range(2)]
            unit_pivot = row_spread(unit, k) * root
            if k < TILE - 1:
                current = [current[i] - masked * pivot[i] for i in range(2)]
                unit = unit - masked * unit_pivot
            pivots.append(pivot)
            unit_pivots.append(unit_pivot)
            if not last:
                factor = below[k] * root
                for j in range(k + 1, TILE):
                    below[j] = below[j] - factor * entries[j]
                for j in range(TILE):
                    diag_n[j] = diag_n[j] - factor * row_spread(factor, j)
                factors.append(factor)
        own = stack_rows(row_in, [pivots[k][half] for k in range(TILE)])
        for k in range(TILE):
            pivots[k][half] = jnp.where(inside, unit_pivots[k], pivots[k][half])
        done = [
            stack_rows(row_in, [pivots[k][i] for k in range(TILE)]) for i in range(2)
        ]
        for i in range(2):
            columns = slice(HALF * i, HALF * i + HALF)
            place = lane + HALF * i
            lower_inverse[rows_t, columns] = jnp.where(
                place < TILE * t + TILE, done[i], 0.0
            )
            shown = jnp.where(inside, own, done[i]) if i == half else done[i]
            upper[rows_t, columns] = jnp.where(place >= TILE * t + row_in, shown, 0.0)
            panel_rows[TILE * (t % PANEL) : TILE * (t % PANEL) + TILE, columns] = (
                jnp.where(
                    (place >= TILE * t + TILE) & (place < TILE * end), 0.0, done[i]
                )
            )
        if not last:
            after[half] = jnp.where(inside, 0.0, after[half])
            for k in range(TILE):
                after = [after[i] - factors[k] * pivots[k][i] for i in range(2)]
            work[rows_n, 0:HALF] = after[0]
            work[rows_n, HALF:ORDER] = after[1]
            diag = diag_n
            stop = min(end + AHEAD, TILES)
            rest = range(t + 2, stop)
            if len(rest) > 0:
                halves = range((TILE * t + 2 * TILE) // HALF, (TILE * stop - 1) // HALF + 1)
                turned = {i: jnp.transpose(done[i]) for i in halves}
                tiles = {}
                for s in rest:
                    rows_s = slice(TILE * s, TILE * s + TILE)
                    tiles[s] = [work[rows_s, 0:HALF], work[rows_s, HALF:ORDER]]
                    tiles[s][half] = jnp.where(inside, 0.0, tiles[s][half])
                for k in range(TILE):
                    for s in rest:
                        i_s, low_s = divmod(TILE * s, HALF)
                        spread = lane_spread(turned[i_s][low_s : low_s + TILE, :], k)
                        tiles[s] = [
                            tiles[s][i] - spread * pivots[k][i] for i in range(2)
                        ]
                for s in rest:
                    rows_s = slice(TILE * s, TILE * s + TILE)
                    work[rows_s, 0:HALF] = tiles[s][0]
                    work[rows_s, HALF:ORDER] = tiles[s][1]
        if t == end - 1 and end + AHEAD < TILES:
            reached = TILE * (end + AHEAD)
            first = TILE * (end - PANEL)
            turned = jnp.transpose(panel_rows[...])
            update = jnp.dot(
                turned[reached:, :],
                panel_rows[...],
                precision=HIGHEST,
                preferred_element_type=F32,
            )
            place = lax.broadcasted_iota(jnp.int32, (ORDER - reached, ORDER), 1)
            in_panel = (place >= first) & (place < TILE * end)
            work[reached:, :] = jnp.where(in_panel, 0.0, work[reached:, :]) - update


def finish_kernel(
    root_total,
    sums_ref,
    weighted,
    basis_hbm,
    factor_hbm,
    coef_hbm,
    work,
    upper,
    inverse,
    panel_rows,
    basis,
    coef,
    sems,
):
    count = coef.shape[0]
    work[0:HALF, :] = sums_ref[0:HALF, :]
    work[HALF:ORDER, HALF:ORDER] = sums_ref[HALF:ORDER, HALF:ORDER]
    work[HALF:ORDER, 0:HALF] = jnp.transpose(sums_ref[0:HALF, HALF:ORDER])
    eliminate(work, upper, inverse, panel_rows)
    copies = [pltpu.make_async_copy(upper, factor_hbm, sems.at[0])]
    copies[0].start()

    def apply(left):
        return lax.dot_general(
            left,
            inverse[...],
            (((1,), (1,)), ((), ())),
            precision=HIGHEST,
            preferred_element_type=F32,
        )

    cross = jnp.concatenate(
        [
            sums_ref[HALF : HALF + count, 0:HALF],
            sums_ref[HALF + count : HALF + 2 * count, 0:HALF],
        ],
        axis=1,
    )
    coef[...] = apply(cross) / F32(root_total)
    copies.append(pltpu.make_async_copy(coef, coef_hbm, sems.at[1]))
    copies[1].start()
    for part in range(basis.shape[0] // ORDER):
        rows = slice(ORDER * part, ORDER * part + ORDER)
        basis[rows, :] = apply(weighted[rows, :])
        copies.append(
            pltpu.make_async_copy(
                basis.at[rows, :], basis_hbm.at[rows, :], sems.at[2 + part]
            )
        )
        copies[-1].start()
    for copy in copies:
        copy.wait()


def per_device(snapshots, volumes, live_rows, probes):
    row_count = snapshots.shape[0]
    count = probes.shape[0]
    total_rows = row_count * CORES * PLANE * DEPTH
    in_vmem = pl.BlockSpec(memory_space=pltpu.VMEM)
    anywhere = pl.BlockSpec(memory_space=pl.ANY)
    volumes = volumes.reshape(1, row_count)
    dma = pltpu.SemaphoreType.DMA

    def reduce_body(*refs):
        reduce_kernel(total_rows, *refs)

    sums, weighted = pl.pallas_call(
        reduce_body,
        out_shape=(
            pltpu.VMEM((ORDER, ORDER), F32),
            pltpu.VMEM((row_count, ORDER), F32),
        ),
        in_specs=[pl.BlockSpec(memory_space=pltpu.HBM)] * 4,
        out_specs=(in_vmem, in_vmem),
        scratch_shapes=[
            pltpu.VMEM((row_count, ORDER), F32),
            pltpu.VMEM((1, row_count), F32),
            pltpu.SMEM((1,), jnp.int32),
            pltpu.VMEM((count, row_count), F32),
            pltpu.VMEM((ORDER, ORDER), F32),
            pltpu.VMEM((HALF, ORDER), F32),
            pltpu.VMEM((PLANE, TILE, ORDER), F32),
            pltpu.VMEM((DEPTH, TILE, ORDER), F32),
            pltpu.VMEM((ORDER, ORDER), F32),
            dma((4,)),
            pltpu.SemaphoreType.REGULAR((len(RELAYS),)),
            dma((2,)),
            dma((3,)),
            dma((3,)),
        ],
        compiler_params=pltpu.CompilerParams(collective_id=0, has_side_effects=True),
        name="reduce_sums",
    )(snapshots, volumes, live_rows, probes)

    def finish_body(*refs):
        finish_kernel(float(total_rows) ** 0.5, *refs)

    return pl.pallas_call(
        finish_body,
        out_shape=(
            jax.ShapeDtypeStruct((row_count, ORDER), F32),
            jax.ShapeDtypeStruct((ORDER, ORDER), F32),
            jax.ShapeDtypeStruct((count, ORDER), F32),
        ),
        in_specs=[in_vmem, in_vmem],
        out_specs=(anywhere, anywhere, anywhere),
        scratch_shapes=[
            pltpu.VMEM((ORDER, ORDER), F32),
            pltpu.VMEM((ORDER, ORDER), F32),
            pltpu.VMEM((ORDER, ORDER), F32),
            pltpu.VMEM((TILE * PANEL, ORDER), F32),
            pltpu.VMEM((row_count, ORDER), F32),
            pltpu.VMEM((count, ORDER), F32),
            dma((2 + row_count // ORDER,)),
        ],
        name="factor_apply",
    )(
        pltpu.with_memory_space_constraint(sums, pltpu.VMEM),
        pltpu.with_memory_space_constraint(weighted, pltpu.VMEM),
    )


def solution(mesh):
    both = ("cells", "sub")
    placed = (P(both, None), P(both), P(both), P(None, both))
    return jax.shard_map(
        per_device,
        mesh=mesh,
        in_specs=placed,
        out_specs=(P(both, None), P(), P()),
        check_vma=False,
    )
```
